32 devices in a mesh: cluster: 8 (over y, x, core), sample: 4 (over z).
Axes of the slice: x: 2, y: 2, z: 4, core: 2. Of those that a mesh axis runs over, the one named last changes fastest.
Arguments:
- child_pattern: float32 [2, 1024, 16384], P(None, 'cluster', 'sample'), may hold values from -6 to 6
- child_local: float32 [2, 1024, 16384], P(None, 'cluster', 'sample'), may hold values from -6 to 6
- interp_weight: float32 [6, 32768], P(None, 'sample'), may hold values from -0.1 to 0.3
- child_phase: float32 [8, 32768], P(None, 'sample'), may hold values from -3.140625 to 3.140625
- translator: float32 [316, 2, 32768], P(None, None, 'sample'), may hold values from -0.6 to 0.6
- partners: int32 [128, 64], replicated, may hold values from 0 to 127
- operator_id: int32 [128, 64], replicated, may hold values from 0 to 315
- list_len: int32 [128], replicated, may hold values from 8 to 64, as said below
Outputs:
- parent_incoming: float32 [2, 128, 32768], P(None, 'cluster', 'sample')
- child_incoming: float32 [2, 1024, 16384], P(None, 'cluster', 'sample')
The draws below stay inside these ranges and needn't reach their ends.
Inputs may be any that keep to these rules, and one draw needn't show every extreme that they name: Parent q's interaction list is its first list_len[q] entries of partners and operator_id; later entries are unused.
All inputs are finite; a program needn't handle non-finite values.
Results may differ from the reference program's by a relative error of at most 0.0003.
Values sent between devices are 32-bit elements; how exact they have to be, the bound alone decides.
No kernel may reach another device: no remote copies, remote signals or barrier semaphores. Data moves between devices by JAX's collectives and lax.ppermute only.
A program may use at most 192 MiB of HBM per device.

```python
import jax
import jax.numpy as jnp
from jax import lax

K1 = 16384
K2 = 32768
TAPS = 6
CHILDREN = 8
NT = 316
LMAX = 64
NP_DEV = 16
NP = 128
NC = 1024


def draw_list_len(key, part):
    key_heavy, key_light, key_long, key_row = jax.random.split(key, 4)
    devices_count = NP // NP_DEV
    heavy_mask = jax.random.randint(key_heavy, (devices_count,), 0, 4) == 0
    heavy_mask = jnp.repeat(heavy_mask, NP_DEV)
    light_len = jax.random.randint(key_light, (NP,), LMAX // 8, LMAX // 4 + 1)
    heavy_len = jax.random.randint(key_long, (NP,), LMAX // 2, LMAX + 1)
    lengths = jnp.where(heavy_mask, heavy_len, light_len)
    forced_row = jax.random.randint(key_row, (), 0, NP)
    return lengths.at[forced_row].set(LMAX).astype(jnp.int32)


def touch_ends(drawn, own_key, low, high):
    extent = drawn.shape
    spot = [jax.random.randint(jax.random.fold_in(own_key, axis), (), 0, extent[axis]) for axis in range(len(extent))]
    drawn = drawn.at[tuple(spot)].set(low)
    longest = extent.index(max(extent))
    spot[longest] = (spot[longest] + 1) % extent[longest]
    return drawn.at[tuple(spot)].set(high)


def levels(own_key, extent, shards, least, largest):
    factor_of, own = 1.0, jax.random.fold_in(own_key, 6)
    for axis_at, blocks in shards:
        heights = jnp.exp(jax.random.uniform(jax.random.fold_in(own, axis_at), (blocks,), jnp.float32, least / len(shards), largest / len(shards)))
        factor_of = factor_of * jnp.repeat(heights, extent[axis_at] // blocks).reshape([-1 if axis == axis_at else 1 for axis in range(len(extent))])
    return factor_of


def gaussian(stream_key, shape, deviation, reach, cuts=(), kind=jnp.bfloat16):
    gain = levels(stream_key, shape, cuts, -0.22, 0.18) if cuts else 1.0
    entries = jax.random.normal(stream_key, shape, jnp.float32) * deviation * gain
    return jnp.minimum(jnp.maximum(entries, -reach), reach).astype(kind)


def setup_inputs(seed: int = 0) -> dict:
    key_of = jax.random.split(jax.random.key(seed), 9)
    child_pattern = gaussian(key_of[0], (2, NC, K1), 1.0, 6.0, ((1, 8), (2, 4)), jnp.float32)
    child_local = gaussian(key_of[1], (2, NC, K1), 1.0, 6.0, ((1, 8), (2, 4)), jnp.float32)
    interp_weight = jnp.clip(-0.1 + 0.4 * jax.random.uniform(key_of[2], (TAPS, K2), jnp.float32) ** levels(key_of[2], (TAPS, K2), ((1, 4),), -0.2, 0.2), -0.1, 0.3)
    child_phase = jnp.clip(jax.random.uniform(key_of[3], (CHILDREN, K2), jnp.float32, -3.140625, 3.140625), -3.140625, 3.140625)
    translator = gaussian(key_of[4], (NT, 2, K2), 0.1, 0.6, ((2, 4),), jnp.float32)
    partners = touch_ends(jax.random.randint(key_of[5], (NP, LMAX), 0, NP), jax.random.fold_in(key_of[5], 1), 0, NP - 1).astype(jnp.int32)
    operator_id = touch_ends(jax.random.randint(key_of[6], (NP, LMAX), 0, NT), jax.random.fold_in(key_of[6], 1), 0, NT - 1).astype(jnp.int32)
    list_len = draw_list_len(jax.random.fold_in(key_of[8], 71), 0)
    return {"child_pattern": child_pattern, "child_local": child_local, "interp_weight": interp_weight, "child_phase": child_phase, "translator": translator, "partners": partners, "operator_id": operator_id, "list_len": list_len}


def upsample_block(children, weight):
    rim_width = TAPS // 2
    base_index = jnp.arange(K2) // 2 - (rim_width - 1)
    total = jnp.zeros((2, children.shape[1], K2), jnp.float32)
    for tap in range(TAPS):
        source_index = ((base_index + tap) % K1).astype(jnp.int32)
        total = total + weight[tap][None, None, :] * jnp.take(children, source_index, axis=2)
    return total


def aggregate(children, weight, cosine, sine):
    upsampled = upsample_block(children, weight).reshape(2, -1, CHILDREN, K2)
    real_part = jnp.sum(cosine[None] * upsampled[0] - sine[None] * upsampled[1], axis=1)
    imag_part = jnp.sum(cosine[None] * upsampled[1] + sine[None] * upsampled[0], axis=1)
    return jnp.stack([real_part, imag_part])


def translate_block(pattern, table, partner_rows, operator_rows, lengths):
    alive_mask = (jnp.arange(LMAX)[None, :] < lengths[:, None]).astype(jnp.float32)
    source = jnp.take(pattern, partner_rows, axis=1)
    coupling = jnp.take(table, operator_rows, axis=0)
    coup_real = coupling[:, :, 0] * alive_mask[:, :, None]
    coup_imag = coupling[:, :, 1] * alive_mask[:, :, None]
    real_part = jnp.sum(coup_real * source[0] - coup_imag * source[1], axis=1)
    imag_part = jnp.sum(coup_real * source[1] + coup_imag * source[0], axis=1)
    return jnp.stack([real_part, imag_part])


def disaggregate(incoming, weight, cosine, sine):
    rim_width = TAPS // 2
    shifted_real = cosine[None] * incoming[0][:, None] + sine[None] * incoming[1][:, None]
    shifted_imag = cosine[None] * incoming[1][:, None] - sine[None] * incoming[0][:, None]
    shifted = jnp.stack([shifted_real, shifted_imag]).reshape(2, -1, K2)
    total = jnp.zeros((2, shifted.shape[1], K1), jnp.float32)
    for tap in range(TAPS):
        paired = (weight[tap][None, None, :] * shifted).reshape(2, shifted.shape[1], K1, 2)
        paired = jnp.sum(paired, axis=3)
        source_index = ((jnp.arange(K1) + rim_width - 1 - tap) % K1).astype(jnp.int32)
        total = total + jnp.take(paired, source_index, axis=2)
    return total


def reference(child_pattern, child_local, interp_weight, child_phase, translator, partners, operator_id, list_len):
    cosine = jnp.cos(child_phase)
    sine = jnp.sin(child_phase)
    blocks = NP // NP_DEV
    grouped = child_pattern.reshape(2, blocks, CHILDREN * NP_DEV, K1).transpose(1, 0, 2, 3)

    def agg_one(children):
        return aggregate(children, interp_weight, cosine, sine)

    parent = lax.map(agg_one, grouped)
    parent = parent.transpose(1, 0, 2, 3).reshape(2, NP, K2)

    def trans_one(item):
        return translate_block(parent, translator, item[0], item[1], item[2])

    rows = (partners.reshape(blocks, NP_DEV, LMAX), operator_id.reshape(blocks, NP_DEV, LMAX), list_len.reshape(blocks, NP_DEV))
    incoming = lax.map(trans_one, rows)
    incoming = incoming.transpose(1, 0, 2, 3).reshape(2, NP, K2)

    def dis_one(block_in):
        return disaggregate(block_in, interp_weight, cosine, sine)

    spread = lax.map(dis_one, incoming.reshape(2, blocks, NP_DEV, K2).transpose(1, 0, 2, 3))
    child_incoming = child_local + spread.transpose(1, 0, 2, 3).reshape(2, NC, K1)
    return incoming, child_incoming
```

```python
import functools

import jax
import jax.numpy as jnp
from jax import lax
from jax.experimental import pallas as pl
from jax.experimental.pallas import tpu as pltpu
from jax.sharding import PartitionSpec as P

TAPS = 6
CHILDREN = 8
LANES = 128
RIM = TAPS // 2
GROUP = 4


def split(values):
    high = values.astype(jnp.bfloat16)
    low = (values - high.astype(jnp.float32)).astype(jnp.bfloat16)
    return high, low


def band(weight):
    rows = lax.broadcasted_iota(jnp.int32, (LANES, 2 * LANES), 0)
    half = lax.broadcasted_iota(jnp.int32, (LANES, 2 * LANES), 1) // 2
    tap = rows - half + (RIM - 1)
    main = jnp.zeros((LANES, 2 * LANES), jnp.float32)
    for w in range(TAPS):
        main = jnp.where(tap == w, weight[w : w + 1, :], main)
    after = tap + LANES
    before = tap - LANES
    rim = jnp.zeros((LANES, 2 * LANES), jnp.float32)
    for w in range(TAPS):
        hit = jnp.where(rows < LANES // 2, after, before) == w
        rim = jnp.where(hit, weight[w : w + 1, :], rim)
    return jnp.concatenate([main, rim], axis=0)


def merge(first, second, step, sub):
    low = (sub & step) == 0
    return jnp.where(low, first, second) + pltpu.roll(jnp.where(low, second, first), step, 0)


def sublane_sums(blocks, sub):
    for step in (1, 2, 4):
        blocks = [merge(blocks[i], blocks[i + 1], step, sub) for i in range(0, len(blocks), 2)]
    return blocks[0]


def aggregate_kernel(base, me_ref, x_ref, left_ref, right_ref, edge_ref, w_ref, c_ref, s_ref, *rest):
    outs, (up_ref,) = rest[:-1], rest[-1:]
    step = pl.program_id(0)
    slices = pl.num_programs(0)
    piece = me_ref[0] ^ (base + step)
    last = me_ref[1] - 1
    blocks = x_ref.shape[2] // LANES
    rows = x_ref.shape[0] * x_ref.shape[1]
    parents = x_ref.shape[1] // CHILDREN
    lane = lax.broadcasted_iota(jnp.int32, (rows, LANES), 1)
    sub = lax.broadcasted_iota(jnp.int32, (8, LANES), 0)
    edge = edge_ref[...].reshape(rows, LANES)
    left = jnp.where(piece == 0, edge, left_ref[...].reshape(rows, LANES))
    right = jnp.where(piece == last, edge, right_ref[...].reshape(rows, LANES))
    parts = [x_ref[:, :, b * LANES : (b + 1) * LANES].reshape(rows, LANES) for b in range(blocks)]
    parts = [split(part) for part in [left] + parts + [right]]
    for b in range(blocks):
        columns = slice(2 * LANES * b, 2 * LANES * (b + 1))
        high, low = split(band(w_ref[:, columns]))
        here, before, after = parts[b + 1], parts[b], parts[b + 2]
        rim = [jnp.where(lane < LANES // 2, after[i], before[i]) for i in range(2)]
        left_hand = jnp.concatenate([here[0], rim[0], here[1], rim[1], here[0], rim[0]], axis=1)
        right_hand = jnp.concatenate([high, high, low], axis=0)
        up_ref[:, columns] = jnp.dot(left_hand, right_hand, preferred_element_type=jnp.float32)

    for i in range(len(outs)):

        @pl.when(step == i)
        def _(out_ref=outs[i]):
            for quad in range(blocks // 2):

                def one(p, carry):
                    gathered = []
                    for b in range(4):
                        col = slice(LANES * (4 * quad + b), LANES * (4 * quad + b + 1))
                        cosine, sine = c_ref[:, col], s_ref[:, col]
                        real = up_ref[pl.ds(p * CHILDREN, CHILDREN), col]
                        imag = up_ref[pl.ds((parents + p) * CHILDREN, CHILDREN), col]
                        gathered.append(cosine * real - sine * imag)
                        gathered.append(cosine * imag + sine * real)
                    out_ref[p, 8 * quad : 8 * quad + 8, :] = sublane_sums(gathered, sub)
                    return carry

                lax.fori_loop(0, parents, one, 0, unroll=2)


def aggregate(me, total, base, count, child, edge, weight, cosine, sine):
    comps, children, width = child.shape
    span = width // total
    blocks = span // LANES
    parents = children // CHILDREN
    where = jnp.stack([me, jnp.int32(total)])
    grid_spec = pltpu.PrefetchScalarGridSpec(
        num_scalar_prefetch=1,
        grid=(count,),
        in_specs=[
            pl.BlockSpec((comps, children, span), lambda g, m: (0, 0, m[0] ^ (base + g))),
            pl.BlockSpec(
                (comps, children, LANES),
                lambda g, m: (0, 0, jnp.maximum((m[0] ^ (base + g)) * blocks - 1, 0)),
            ),
            pl.BlockSpec(
                (comps, children, LANES),
                lambda g, m: (0, 0, jnp.minimum(((m[0] ^ (base + g)) + 1) * blocks, total * blocks - 1)),
            ),
            pl.BlockSpec((comps, children, LANES), lambda g, m: (0, 0, 0)),
            pl.BlockSpec((TAPS, 2 * span), lambda g, m: (0, m[0] ^ (base + g))),
            pl.BlockSpec((CHILDREN, 2 * span), lambda g, m: (0, m[0] ^ (base + g))),
            pl.BlockSpec((CHILDREN, 2 * span), lambda g, m: (0, m[0] ^ (base + g))),
        ],
        out_specs=[pl.BlockSpec((parents, 4 * blocks, LANES), lambda g, m: (0, 0, 0))] * count,
        scratch_shapes=[pltpu.VMEM((comps * children, 2 * span), jnp.float32)],
    )
    return pl.pallas_call(
        functools.partial(aggregate_kernel, base),
        grid_spec=grid_spec,
        out_shape=[jax.ShapeDtypeStruct((parents, 4 * blocks, LANES), jnp.float32)] * count,
        name="aggregate",
        cost_estimate=pl.CostEstimate(flops=4 << 30, bytes_accessed=6 << 20, transcendentals=0),
    )(where, child, child, child, edge, weight, cosine, sine)


def translate_kernel(base, count, me_ref, partner_ref, op_ref, len_ref, table_ref, *rest):
    total = me_ref.shape[0]
    sources, outs = rest[:total], rest[total : total + count]
    held, swapped = rest[total + count :]
    parents, rows, _ = sources[0].shape
    me = me_ref[0]
    odd = (lax.broadcasted_iota(jnp.int32, (rows, LANES), 0) & 1) == 1
    for k in range(total):
        first = (me ^ k) * parents

        def place(p, carry, k=k, first=first):
            block = sources[k][p]
            held[first + p] = block
            swapped[first + p] = jnp.where(odd, pltpu.roll(block, 1, 0), pltpu.roll(block, rows - 1, 0))
            return carry

        lax.fori_loop(0, parents, place, 0, unroll=4)

    for i in range(count):
        first = (me ^ (base + i)) * parents

        def receive(q, carry, out_ref=outs[i], first=first):
            row = first + q

            def add(step, totals):
                direct, crossed = totals
                for u in range(GROUP):
                    slot = step * GROUP + u
                    operator = table_ref[op_ref[row, slot]]
                    partner = partner_ref[row, slot]
                    direct = direct + operator * held[partner]
                    crossed = crossed + operator * swapped[partner]
                return direct, crossed

            zero = jnp.zeros((rows, LANES), jnp.float32)
            direct, crossed = lax.fori_loop(0, (len_ref[row] + GROUP - 1) // GROUP, add, (zero, zero))
            real = direct - pltpu.roll(direct, rows - 1, 0)
            imag = crossed + pltpu.roll(crossed, 1, 0)
            out_ref[q] = jnp.where(odd, imag, real)
            return carry

        lax.fori_loop(0, parents, receive, 0)


def translate(me, base, count, partners, operators, lengths, table, sources):
    total = len(sources)
    parents, rows, lanes = sources[0].shape
    smem = pl.BlockSpec(memory_space=pltpu.SMEM)
    vmem = pl.BlockSpec(memory_space=pltpu.VMEM)
    return pl.pallas_call(
        functools.partial(translate_kernel, base, count),
        in_specs=[smem] * 4 + [vmem] * (1 + total),
        out_specs=[vmem] * count,
        out_shape=[jax.ShapeDtypeStruct((parents, rows, lanes), jnp.float32)] * count,
        scratch_shapes=[pltpu.VMEM((total * parents, rows, lanes), jnp.float32)] * 2,
        name="translate",
        cost_estimate=pl.CostEstimate(flops=4 << 30, bytes_accessed=4 << 20, transcendentals=0),
    )(jnp.full((total,), me, jnp.int32), partners, operators, lengths, table, *sources)


def spread_kernel(me_ref, local_ref, w_ref, wn_ref, c_ref, cn_ref, s_ref, sn_ref, *rest):
    total = me_ref.shape[0]
    sources = rest[:total]
    incoming_ref, out_ref, first_ref, last_ref = rest[total : total + 4]
    fields, shifted, carried, trailing = rest[total + 4 :]
    parents, rows_of, _ = sources[0].shape
    blocks = rows_of // 4
    comps, children, _ = out_ref.shape
    rows = comps * children
    step = pl.program_id(0)
    me = me_ref[0]
    lane = lax.broadcasted_iota(jnp.int32, (rows, LANES), 1)

    @pl.when(step == 0)
    def _():
        for k in range(total):
            fields[me ^ k] = sources[k][...].reshape(parents * rows_of, LANES)

    for b in range(2 * blocks):
        for comp in range(comps):
            for half in range(parents // 8):
                incoming_ref[comp, 8 * half : 8 * half + 8, b * LANES : (b + 1) * LANES] = fields[
                    step, pl.ds(8 * half * rows_of + 2 * b + comp, 8, stride=rows_of), :
                ]

    def block(piece, index, weight, cos_ref, sin_ref):
        for half in range(2):
            b = 2 * index + half
            columns = slice(LANES * b, LANES * (b + 1))
            cosine, sine = cos_ref[:, columns], sin_ref[:, columns]

            def one(p, carry):
                at = p * rows_of + 2 * b
                real = jnp.broadcast_to(fields[piece, pl.ds(at, 1), :], (CHILDREN, LANES))
                imag = jnp.broadcast_to(fields[piece, pl.ds(at + 1, 1), :], (CHILDREN, LANES))
                into = slice(half * LANES, (half + 1) * LANES)
                shifted[pl.ds(p * CHILDREN, CHILDREN), into] = cosine * real + sine * imag
                shifted[pl.ds((parents + p) * CHILDREN, CHILDREN), into] = cosine * imag - sine * real
                return carry

            lax.fori_loop(0, parents, one, 0, unroll=4)
        high, low = split(shifted[...])
        whigh, wlow = split(band(weight))
        left_hand = jnp.concatenate([high, low, high], axis=1)
        right_hand = jnp.concatenate([whigh, whigh, wlow], axis=1)
        both = lax.dot_general(
            left_hand, right_hand, (((1,), (1,)), ((), ())), preferred_element_type=jnp.float32
        )
        return both[:, :LANES], both[:, LANES:]

    @pl.when(step == 0)
    def _():
        main, rim = block(0, 0, w_ref[:, : 2 * LANES], c_ref, s_ref)
        carried[0] = main
        carried[1] = rim
        trailing[...] = jnp.zeros((rows, LANES), jnp.float32)
        first_ref[...] = rim.reshape(comps, children, LANES)

    def finish(index, main, before, after):
        columns = slice(LANES * index, LANES * (index + 1))
        value = main + jnp.where(lane < LANES // 2, before, after)
        out_ref[:, :, columns] = local_ref[:, :, columns] + value.reshape(comps, children, LANES)

    for b in range(1, blocks):
        main, rim = block(step, b, w_ref[:, 2 * LANES * b : 2 * LANES * (b + 1)], c_ref, s_ref)
        finish(b - 1, carried[0], trailing[...], rim)
        trailing[...] = carried[1]
        carried[0] = main
        carried[1] = rim

    @pl.when(step < total - 1)
    def _():
        main, rim = block(step + 1, 0, wn_ref[...], cn_ref, sn_ref)
        finish(blocks - 1, carried[0], trailing[...], rim)
        trailing[...] = carried[1]
        carried[0] = main
        carried[1] = rim

    @pl.when(step == total - 1)
    def _():
        finish(blocks - 1, carried[0], trailing[...], jnp.zeros((rows, LANES), jnp.float32))
        last_ref[...] = carried[1].reshape(comps, children, LANES)


def spread(me, child_local, weight, cosine, sine, sources):
    total = len(sources)
    parents, rows_of, _ = sources[0].shape
    comps, children, width = child_local.shape
    span = width // total
    blocks = span // LANES
    smem = pl.BlockSpec(memory_space=pltpu.SMEM)
    held = pl.BlockSpec((parents, rows_of, LANES), lambda g: (0, 0, 0))
    edge = pl.BlockSpec((comps, children, LANES), lambda g: (0, 0, 0))

    def after(g):
        return (0, jnp.minimum((g + 1) * blocks, total * blocks - 1))

    return pl.pallas_call(
        spread_kernel,
        grid=(total,),
        in_specs=[
            smem,
            pl.BlockSpec((comps, children, span), lambda g: (0, 0, g)),
            pl.BlockSpec((TAPS, 2 * span), lambda g: (0, g)),
            pl.BlockSpec((TAPS, 2 * LANES), after),
            pl.BlockSpec((CHILDREN, 2 * span), lambda g: (0, g)),
            pl.BlockSpec((CHILDREN, 2 * LANES), after),
            pl.BlockSpec((CHILDREN, 2 * span), lambda g: (0, g)),
            pl.BlockSpec((CHILDREN, 2 * LANES), after),
        ]
        + [held] * total,
        out_specs=[
            pl.BlockSpec((comps, parents, 2 * span), lambda g: (0, 0, g)),
            pl.BlockSpec((comps, children, span), lambda g: (0, 0, g)),
            edge,
            edge,
        ],
        out_shape=[
            jax.ShapeDtypeStruct((comps, parents, 2 * width), jnp.float32),
            jax.ShapeDtypeStruct((comps, children, width), jnp.float32),
            jax.ShapeDtypeStruct((comps, children, LANES), jnp.float32),
            jax.ShapeDtypeStruct((comps, children, LANES), jnp.float32),
        ],
        scratch_shapes=[
            pltpu.VMEM((total, parents * rows_of, LANES), jnp.float32),
            pltpu.VMEM((comps * children, 2 * LANES), jnp.float32),
            pltpu.VMEM((2, comps * children, LANES), jnp.float32),
            pltpu.VMEM((comps * children, LANES), jnp.float32),
        ],
        name="spread",
        cost_estimate=pl.CostEstimate(flops=8 << 30, bytes_accessed=12 << 20, transcendentals=0),
    )(
        jnp.full((total,), me, jnp.int32),
        child_local,
        weight,
        weight,
        cosine,
        cosine,
        sine,
        sine,
        *sources,
    )


def ring(count):
    forward = [(i, (i + 1) % count) for i in range(count)]
    return forward, [(target, source) for source, target in forward]


def fast(
    child_pattern,
    child_local,
    interp_weight,
    child_phase,
    translator,
    partners,
    operator_id,
    list_len,
):
    total = lax.axis_size("cluster")
    me = lax.axis_index("cluster")
    comps, children, width = child_pattern.shape
    forward, backward = ring(lax.axis_size("sample"))
    low = lax.ppermute(child_pattern[:, :, width - (RIM - 1) :], "sample", forward)
    high = lax.ppermute(child_pattern[:, :, :RIM], "sample", backward)
    gap = jnp.zeros((comps, children, LANES - TAPS + 1), jnp.float32)
    edge = jnp.concatenate([high, gap, low], axis=2)
    cosine = jnp.cos(child_phase)
    sine = jnp.sin(child_phase)

    def swap(block, k):
        if k == 0:
            return block
        return lax.ppermute(block, "cluster", [(i, i ^ k) for i in range(total)])

    half = total // 2
    sent = [None] * total
    for base in (half, 0):
        made = aggregate(me, total, base, half, child_pattern, edge, interp_weight, cosine, sine)
        for i in range(half):
            sent[base + i] = made[i]
    sources = [swap(sent[k], k) for k in range(total)]

    count, _, samples = translator.shape
    table = translator.reshape(count, comps, samples // LANES, LANES).transpose(0, 2, 1, 3)
    table = table.reshape(count, 2 * samples // LANES, LANES)
    rows = 2 * samples // LANES // total
    table = lax.dynamic_slice_in_dim(table, me * rows, rows, 1)
    table = jnp.pad(table, ((0, 1), (0, 0), (0, 0)))
    alive = jnp.arange(operator_id.shape[1])[None, :] < list_len[:, None]
    operators = jnp.where(alive, operator_id, count)
    back = [None] * total
    for base in (half, 0):
        made = translate(me, base, half, partners, operators, list_len, table, sources)
        for i in range(half):
            back[base + i] = made[i]
    fields = [swap(back[k], k) for k in range(total)]
    incoming, child_incoming, first, last = spread(
        me, child_local, interp_weight, cosine, sine, fields
    )
    low = lax.ppermute(last[:, :, :RIM], "sample", forward)
    high = lax.ppermute(first[:, :, LANES - RIM + 1 :], "sample", backward)
    child_incoming = child_incoming.at[:, :, :RIM].add(low)
    child_incoming = child_incoming.at[:, :, width - RIM + 1 :].add(high)
    return incoming, child_incoming


def with_halo(block, sides, width):
    for axis, dim in sides:
        forward, backward = ring(lax.axis_size(axis))
        low = lax.ppermute(
            lax.slice_in_dim(block, block.shape[dim] - width, None, axis=dim), axis, forward
        )
        high = lax.ppermute(lax.slice_in_dim(block, 0, width, axis=dim), axis, backward)
        block = jnp.concatenate([low, block, high], axis=dim)
    return block


def translate_rows(pattern, table, partner_rows, operator_rows, lengths):
    receivers = partner_rows.shape[0]
    slot_count = partner_rows.shape[1]
    group_size = 16
    sample_count = pattern.shape[2]

    def advance(block, total):
        partner_cols = lax.dynamic_slice_in_dim(partner_rows, block * group_size, group_size, 1)
        operator_cols = lax.dynamic_slice_in_dim(operator_rows, block * group_size, group_size, 1)
        slot_index = block * group_size + jnp.arange(group_size)
        alive_mask = (slot_index[None, :] < lengths[:, None]).astype(jnp.float32)
        source = jnp.take(pattern, partner_cols, axis=1)
        coupling = jnp.take(table, operator_cols, axis=0)
        coup_real = coupling[:, :, 0] * alive_mask[:, :, None]
        coup_imag = coupling[:, :, 1] * alive_mask[:, :, None]
        real_part = jnp.sum(coup_real * source[0] - coup_imag * source[1], axis=1)
        imag_part = jnp.sum(coup_real * source[1] + coup_imag * source[0], axis=1)
        return total + jnp.stack([real_part, imag_part])

    start_total = jnp.zeros((2, receivers, sample_count), jnp.float32)
    return lax.fori_loop(0, slot_count // group_size, advance, start_total)


def phase_sum(upsampled, cosine, sine, parent_count):
    grouped = upsampled.reshape(2, parent_count, CHILDREN, upsampled.shape[2])
    real_part = jnp.sum(cosine[None] * grouped[0] - sine[None] * grouped[1], axis=1)
    imag_part = jnp.sum(cosine[None] * grouped[1] + sine[None] * grouped[0], axis=1)
    return jnp.stack([real_part, imag_part])


def phase_spread(incoming, cosine, sine):
    shifted_real = cosine[None] * incoming[0][:, None] + sine[None] * incoming[1][:, None]
    shifted_imag = cosine[None] * incoming[1][:, None] - sine[None] * incoming[0][:, None]
    return jnp.stack([shifted_real, shifted_imag]).reshape(2, -1, incoming.shape[2])


def plain(
    child_pattern,
    child_local,
    interp_weight,
    child_phase,
    translator,
    partners,
    operator_id,
    list_len,
):
    rim_width = TAPS // 2
    child_count = child_pattern.shape[1]
    parent_count = child_count // CHILDREN
    half_samples = child_pattern.shape[2]
    cosine = jnp.cos(child_phase)
    sine = jnp.sin(child_phase)
    cos_even = cosine[:, 0::2]
    cos_odd = cosine[:, 1::2]
    sin_even = sine[:, 0::2]
    sin_odd = sine[:, 1::2]
    weight_even = interp_weight[:, 0::2]
    weight_odd = interp_weight[:, 1::2]
    padded = with_halo(child_pattern, (("sample", 2),), rim_width)
    up_even = jnp.zeros((2, child_count, half_samples), jnp.float32)
    up_odd = jnp.zeros((2, child_count, half_samples), jnp.float32)
    for tap in range(TAPS):
        window = padded[:, :, 1 + tap : 1 + tap + half_samples]
        up_even = up_even + weight_even[tap][None, None, :] * window
        up_odd = up_odd + weight_odd[tap][None, None, :] * window
    parent_even = phase_sum(up_even, cos_even, sin_even, parent_count)
    parent_odd = phase_sum(up_odd, cos_odd, sin_odd, parent_count)
    parent = jnp.stack([parent_even, parent_odd], axis=3).reshape(2, parent_count, 2 * half_samples)
    cluster_index = lax.axis_index("cluster")
    whole = lax.all_gather(parent, "cluster", axis=1, tiled=True)
    first_row = cluster_index * parent_count
    own_partners = lax.dynamic_slice_in_dim(partners, first_row, parent_count, 0)
    own_operators = lax.dynamic_slice_in_dim(operator_id, first_row, parent_count, 0)
    own_lengths = lax.dynamic_slice_in_dim(list_len, first_row, parent_count, 0)
    incoming = translate_rows(whole, translator, own_partners, own_operators, own_lengths)
    shift_even = phase_spread(incoming[:, :, 0::2], cos_even, sin_even)
    shift_odd = phase_spread(incoming[:, :, 1::2], cos_odd, sin_odd)
    weighted = jnp.stack(
        [
            weight_even[tap][None, None, :] * shift_even
            + weight_odd[tap][None, None, :] * shift_odd
            for tap in range(TAPS)
        ]
    )
    padded_weighted = with_halo(weighted, (("sample", 3),), rim_width)
    child_incoming = child_local
    for tap in range(TAPS):
        offset = 2 * rim_width - 1 - tap
        child_incoming = child_incoming + padded_weighted[tap, :, :, offset : offset + half_samples]
    return (incoming, child_incoming)


def local(child_pattern, *rest):
    total = lax.axis_size("cluster")
    share = child_pattern.shape[2] // total
    fits = total & (total - 1) == 0 and share >= 2 * LANES and share % (2 * LANES) == 0
    fits = fits and share * total == child_pattern.shape[2]
    return (fast if fits else plain)(child_pattern, *rest)


def solution(mesh):
    placed = (
        P(None, "cluster", "sample"),
        P(None, "cluster", "sample"),
        P(None, "sample"),
        P(None, "sample"),
        P(None, None, "sample"),
        P(),
        P(),
        P(),
    )
    return jax.shard_map(
        local,
        mesh=mesh,
        in_specs=placed,
        out_specs=(P(None, "cluster", "sample"), P(None, "cluster", "sample")),
        check_vma=False,
    )
```

```python
import functools

import jax
import jax.numpy as jnp
from jax import lax
from jax.experimental import pallas as pl
from jax.experimental.pallas import tpu as pltpu
from jax.sharding import PartitionSpec as P

TAPS = 6
CHILDREN = 8
LANES = 128
RIM = TAPS // 2
GROUP = 4
UNROLL = 4


def split(values):
    high = values.astype(jnp.bfloat16)
    low = (values - high.astype(jnp.float32)).astype(jnp.bfloat16)
    return high, low


def contract(left, right, dims):
    (lh, ll), (rh, rl) = left, right
    axis_l, axis_r = dims
    return lax.dot_general(
        jnp.concatenate([lh, ll, lh], axis=axis_l),
        jnp.concatenate([rh, rh, rl], axis=axis_r),
        (((axis_l,), (axis_r,)), ((), ())),
        preferred_element_type=jnp.float32,
    )


def turn(phase):
    half = 0.5 * phase
    square = half * half
    sine = jnp.full_like(square, -1.0 / 39916800)
    for term in (1.0 / 362880, -1.0 / 5040, 1.0 / 120, -1.0 / 6, 1.0):
        sine = sine * square + term
    sine = sine * half
    cosine = jnp.full_like(square, 1.0 / 479001600)
    for term in (-1.0 / 3628800, 1.0 / 40320, -1.0 / 720, 1.0 / 24, -0.5, 1.0):
        cosine = cosine * square + term
    double = sine + sine
    return 1.0 - double * sine, double * cosine


def tap_rows():
    row = lax.broadcasted_iota(jnp.int32, (8, LANES), 0)
    half = lax.broadcasted_iota(jnp.int32, (8, LANES), 1) // 2
    near = row - half + (RIM - 1)
    picks = []
    for tile in range(-1, LANES // 16 + 1):
        tap = near + 8 * tile
        picks.append(jnp.where((tap >= 0) & (tap < TAPS), tap, TAPS))
    return picks


def band_tiles(weight, picks):
    padded = jnp.concatenate([weight, jnp.zeros((8 - TAPS, LANES), jnp.float32)], axis=0)
    return [
        jnp.take_along_axis(padded, pick, axis=0, mode="promise_in_bounds") for pick in picks
    ]


def band(weight, picks):
    high = weight.astype(jnp.bfloat16).astype(jnp.float32)
    parts = []
    zero = jnp.zeros((8, LANES), jnp.float32)
    inner = LANES // 16
    for piece in (high, weight - high):
        first = band_tiles(piece[:, :LANES], picks)
        second = band_tiles(piece[:, LANES:], picks)
        left = first[1:] + [zero] * (inner - 1) + [zero] * (2 * inner - 1) + [first[0]]
        right = [zero] * (inner - 1) + second[:-1] + [second[-1]] + [zero] * (2 * inner - 1)
        columns = [jnp.concatenate(tiles, axis=0).astype(jnp.bfloat16) for tiles in (left, right)]
        parts.append(jnp.concatenate(columns, axis=1))
    return tuple(parts)


def picker(first, rows):
    row = lax.broadcasted_iota(jnp.int32, (rows, LANES), 0)
    lane = lax.broadcasted_iota(jnp.int32, (rows, LANES), 1)
    return (lane == row + first).astype(jnp.bfloat16)


def merge(first, second, step, sub):
    low = (sub & step) == 0
    return jnp.where(low, first, second) + pltpu.roll(jnp.where(low, second, first), step, 0)


def sublane_sums(blocks, sub):
    for step in (1, 2, 4):
        blocks = [merge(blocks[i], blocks[i + 1], step, sub) for i in range(0, len(blocks), 2)]
    return blocks[0]


def rim_kernel(first_ref, last_ref, low_ref, high_ref):
    rows = first_ref.shape[0] * first_ref.shape[1]
    for source, target, at in ((first_ref, low_ref, 0), (last_ref, high_ref, LANES - 8)):
        pick = picker(at, 8)
        high, low = split(source[...].reshape(rows, LANES))
        target[...] = lax.dot_general(
            jnp.concatenate([pick, pick], axis=1),
            jnp.concatenate([high, low], axis=1),
            (((1,), (1,)), ((), ())),
            preferred_element_type=jnp.float32,
        )


def rims(child):
    comps, children, width = child.shape
    rows = comps * children
    return pl.pallas_call(
        rim_kernel,
        grid=(1,),
        in_specs=[
            pl.BlockSpec((comps, children, LANES), lambda g: (0, 0, 0)),
            pl.BlockSpec((comps, children, LANES), lambda g: (0, 0, width // LANES - 1)),
        ],
        out_specs=[pl.BlockSpec((8, rows), lambda g: (0, 0))] * 2,
        out_shape=[jax.ShapeDtypeStruct((8, rows), jnp.float32)] * 2,
        name="rims",
        cost_estimate=pl.CostEstimate(flops=1 << 20, bytes_accessed=1 << 18, transcendentals=0),
    )(child, child)


def widen(compact, at):
    high, low = split(compact)
    pick = picker(at, 8)
    return lax.dot_general(
        jnp.concatenate([high, low], axis=0),
        jnp.concatenate([pick, pick], axis=0),
        (((0,), (0,)), ((), ())),
        preferred_element_type=jnp.float32,
    )


def aggregate_kernel(base, me_ref, x_ref, left_ref, right_ref, before_ref, after_ref, w_ref, f_ref, *rest):
    outs, (edge_ref, turn_ref, up_ref) = rest[:-3], rest[-3:]
    step = pl.program_id(0)
    piece = me_ref[0] ^ (base + step)
    last = me_ref[1] - 1
    blocks = x_ref.shape[2] // LANES
    rows = x_ref.shape[0] * x_ref.shape[1]
    parents = x_ref.shape[1] // CHILDREN
    lane = lax.broadcasted_iota(jnp.int32, (rows, LANES), 1)
    sub = lax.broadcasted_iota(jnp.int32, (8, LANES), 0)
    picks = tap_rows()
    edge_ref[0] = left_ref[...].reshape(rows, LANES)
    edge_ref[1] = right_ref[...].reshape(rows, LANES)

    @pl.when(piece == 0)
    def _():
        edge_ref[0] = widen(before_ref[...], LANES - 8)

    @pl.when(piece == last)
    def _():
        edge_ref[1] = widen(after_ref[...], 0)

    turn_ref[0], turn_ref[1] = turn(f_ref[...])
    parts = [x_ref[:, :, b * LANES : (b + 1) * LANES].reshape(rows, LANES) for b in range(blocks)]
    parts = [split(part) for part in [edge_ref[0]] + parts + [edge_ref[1]]]
    for b in range(blocks):
        columns = slice(2 * LANES * b, 2 * LANES * (b + 1))
        here, before, after = parts[b + 1], parts[b], parts[b + 2]
        rim = [jnp.where(lane < LANES // 2, after[i], before[i]) for i in range(2)]
        left_hand = [jnp.concatenate([here[i], rim[i]], axis=1) for i in range(2)]
        up_ref[:, columns] = contract(left_hand, band(w_ref[:, columns], picks), (1, 0))

    for i in range(len(outs)):

        @pl.when(step == i)
        def _(out_ref=outs[i]):
            for quad in range(blocks // 2):

                def one(p, carry):
                    gathered = []
                    for b in range(4):
                        col = slice(LANES * (4 * quad + b), LANES * (4 * quad + b + 1))
                        cosine, sine = turn_ref[0, :, col], turn_ref[1, :, col]
                        real = up_ref[pl.ds(p * CHILDREN, CHILDREN), col]
                        imag = up_ref[pl.ds((parents + p) * CHILDREN, CHILDREN), col]
                        gathered.append(cosine * real - sine * imag)
                        gathered.append(cosine * imag + sine * real)
                    out_ref[p, 8 * quad : 8 * quad + 8, :] = sublane_sums(gathered, sub)
                    return carry

                lax.fori_loop(0, parents, one, 0, unroll=4)


def aggregate(me, total, base, count, child, before, after, weight, phase):
    comps, children, width = child.shape
    span = width // total
    blocks = span // LANES
    parents = children // CHILDREN
    rows = comps * children
    where = jnp.stack([me, jnp.int32(total)])

    def left(g, m):
        return (0, 0, jnp.maximum((m[0] ^ (base + g)) * blocks - 1, 0))

    def right(g, m):
        return (0, 0, jnp.minimum(((m[0] ^ (base + g)) + 1) * blocks, total * blocks - 1))

    grid_spec = pltpu.PrefetchScalarGridSpec(
        num_scalar_prefetch=1,
        grid=(count,),
        in_specs=[
            pl.BlockSpec((comps, children, span), lambda g, m: (0, 0, m[0] ^ (base + g))),
            pl.BlockSpec((comps, children, LANES), left),
            pl.BlockSpec((comps, children, LANES), right),
            pl.BlockSpec((8, rows), lambda g, m: (0, 0)),
            pl.BlockSpec((8, rows), lambda g, m: (0, 0)),
            pl.BlockSpec((TAPS, 2 * span), lambda g, m: (0, m[0] ^ (base + g))),
            pl.BlockSpec((CHILDREN, 2 * span), lambda g, m: (0, m[0] ^ (base + g))),
        ],
        out_specs=[pl.BlockSpec((parents, 4 * blocks, LANES), lambda g, m: (0, 0, 0))] * count,
        scratch_shapes=[
            pltpu.VMEM((2, rows, LANES), jnp.float32),
            pltpu.VMEM((2, CHILDREN, 2 * span), jnp.float32),
            pltpu.VMEM((rows, 2 * span), jnp.float32),
        ],
    )
    return pl.pallas_call(
        functools.partial(aggregate_kernel, base),
        grid_spec=grid_spec,
        out_shape=[jax.ShapeDtypeStruct((parents, 4 * blocks, LANES), jnp.float32)] * count,
        name="aggregate",
        cost_estimate=pl.CostEstimate(flops=4 << 30, bytes_accessed=6 << 20, transcendentals=0),
    )(where, child, child, child, before, after, weight, phase)


def translate_kernel(slots, me_ref, partner_ref, op_ref, len_ref, table_ref, *rest):
    total = me_ref.shape[0]
    sources, outs = rest[:total], rest[total : 2 * total]
    held, sums = rest[2 * total :]
    parents, rows, _ = sources[0].shape
    table = table_ref.reshape(table_ref.shape[0] * rows, LANES)
    me = me_ref[0]
    odd = (lax.broadcasted_iota(jnp.int32, (rows, LANES), 0) & 1) == 1
    for k in range(total):
        first = (me ^ k) * parents

        def place(p, carry, k=k, first=first):
            block = sources[k][p]
            at = pl.multiple_of((first + p) * 2 * rows, 2 * rows)
            held[pl.ds(at, rows), :] = block
            held[pl.ds(at + rows, rows), :] = jnp.where(
                odd, pltpu.roll(block, 1, 0), pltpu.roll(block, rows - 1, 0)
            )
            return carry

        lax.fori_loop(0, parents, place, 0, unroll=4)

    for i in range(total):
        first = (me ^ i) * parents
        groups = jnp.int32(0)
        for q in range(parents):
            groups = groups + (len_ref[first + q] + GROUP - 1) // GROUP

        def add(step, state, first=first):
            row, slot, totals = state
            for _ in range(UNROLL):
                keep = jnp.where(slot > 0, 1.0, 0.0).astype(jnp.float32)
                at = (first + row) * slots + slot
                direct, crossed = [], []
                for u in range(GROUP):
                    operator = table[pl.ds(pl.multiple_of(op_ref[at + u], rows), rows), :]
                    partner = pl.multiple_of(partner_ref[at + u], 2 * rows)
                    direct.append(operator * held[pl.ds(partner, rows), :])
                    crossed.append(operator * held[pl.ds(partner + rows, rows), :])
                while len(direct) > 1:
                    direct = [a + b for a, b in zip(direct[::2], direct[1::2])]
                    crossed = [a + b for a, b in zip(crossed[::2], crossed[1::2])]
                totals = (totals[0] * keep + direct[0], totals[1] * keep + crossed[0])
                sums[row, :rows, :] = totals[0]
                sums[row, rows:, :] = totals[1]
                slot = slot + GROUP
                done = slot >= len_ref[first + row]
                row = jnp.where(done, row + 1, row)
                slot = jnp.where(done, 0, slot)
            return row, slot, totals

        zero = jnp.zeros((rows, LANES), jnp.float32)
        lax.fori_loop(
            0, (groups + UNROLL - 1) // UNROLL, add, (jnp.int32(0), jnp.int32(0), (zero, zero))
        )

        def combine(q, carry, out_ref=outs[i]):
            direct, crossed = sums[q, :rows, :], sums[q, rows:, :]
            real = direct - pltpu.roll(direct, rows - 1, 0)
            imag = crossed + pltpu.roll(crossed, 1, 0)
            out_ref[q] = jnp.where(odd, imag, real)
            return carry

        lax.fori_loop(0, parents, combine, 0, unroll=4)


def translate(me, partners, operators, lengths, slots, table, sources):
    total = len(sources)
    parents, rows, lanes = sources[0].shape
    smem = pl.BlockSpec(memory_space=pltpu.SMEM)
    vmem = pl.BlockSpec(memory_space=pltpu.VMEM)
    return pl.pallas_call(
        functools.partial(translate_kernel, slots),
        in_specs=[smem] * 4 + [vmem] * (1 + total),
        out_specs=[vmem] * total,
        out_shape=[jax.ShapeDtypeStruct((parents, rows, lanes), jnp.float32)] * total,
        scratch_shapes=[
            pltpu.VMEM((total * parents * 2 * rows, lanes), jnp.float32),
            pltpu.VMEM((parents + UNROLL, 2 * rows, lanes), jnp.float32),
        ],
        name="translate",
        cost_estimate=pl.CostEstimate(flops=4 << 30, bytes_accessed=4 << 20, transcendentals=0),
    )(jnp.full((total,), me, jnp.int32), partners, operators, lengths, table, *sources)


def shift(field, at, cosine, sine):
    real = jnp.broadcast_to(field[pl.ds(at, 1), :], (CHILDREN, LANES))
    imag = jnp.broadcast_to(field[pl.ds(at + 1, 1), :], (CHILDREN, LANES))
    return cosine * real + sine * imag, cosine * imag - sine * real


def shift_all(field, b, cosine, sine, parents, rows_of):
    pairs = [shift(field, p * rows_of + 2 * b, cosine, sine) for p in range(parents)]
    return jnp.concatenate([pair[0] for pair in pairs] + [pair[1] for pair in pairs], axis=0)


def outer_kernel(me_ref, wf_ref, wl_ref, ff_ref, fl_ref, *rest):
    total = me_ref.shape[0]
    sources, (low_ref, high_ref, field) = rest[:total], rest[total:]
    parents, rows_of, _ = sources[0].shape
    me = me_ref[0]
    picks = tap_rows()
    for piece, w_ref, f_ref, out_ref, tile, b in (
        (0, wf_ref, ff_ref, low_ref, 0, 0),
        (total - 1, wl_ref, fl_ref, high_ref, -1, rows_of // 2 - 1),
    ):
        for k in range(total):

            @pl.when(me ^ k == piece)
            def _(k=k):
                field[...] = sources[k][...].reshape(parents * rows_of, LANES)

        cosine, sine = turn(f_ref[...])
        shifted = shift_all(field, b, cosine, sine, parents, rows_of)
        taps = band_tiles(w_ref[...], picks)[tile]
        out_ref[...] = contract(split(taps), split(shifted), (1, 1))


def outer(me, weight, phase, sources):
    total = len(sources)
    parents, rows_of, _ = sources[0].shape
    samples = weight.shape[1]
    rows = 2 * parents * CHILDREN
    smem = pl.BlockSpec(memory_space=pltpu.SMEM)
    held = pl.BlockSpec((parents, rows_of, LANES), lambda g: (0, 0, 0))
    end = samples // LANES - 1
    return pl.pallas_call(
        outer_kernel,
        grid=(1,),
        in_specs=[
            smem,
            pl.BlockSpec((TAPS, LANES), lambda g: (0, 0)),
            pl.BlockSpec((TAPS, LANES), lambda g: (0, end)),
            pl.BlockSpec((CHILDREN, LANES), lambda g: (0, 0)),
            pl.BlockSpec((CHILDREN, LANES), lambda g: (0, end)),
        ]
        + [held] * total,
        out_specs=[pl.BlockSpec((8, rows), lambda g: (0, 0))] * 2,
        out_shape=[jax.ShapeDtypeStruct((8, rows), jnp.float32)] * 2,
        scratch_shapes=[pltpu.VMEM((parents * rows_of, LANES), jnp.float32)],
        name="outer",
        cost_estimate=pl.CostEstimate(flops=1 << 24, bytes_accessed=1 << 20, transcendentals=0),
    )(jnp.full((total,), me, jnp.int32), weight, weight, phase, phase, *sources)


def spread_kernel(me_ref, local_ref, w_ref, wn_ref, f_ref, fn_ref, *rest):
    total = me_ref.shape[0]
    sources = rest[:total]
    incoming_ref, out_ref = rest[total : total + 2]
    fields, carried = rest[total + 2 :]
    parents, rows_of, _ = sources[0].shape
    blocks = rows_of // 4
    comps, children, _ = out_ref.shape
    rows = comps * children
    step = pl.program_id(0)
    me = me_ref[0]
    lane = lax.broadcasted_iota(jnp.int32, (rows, LANES), 1)
    picks = tap_rows()

    @pl.when(step == 0)
    def _():
        for k in range(total):
            fields[me ^ k] = sources[k][...].reshape(parents * rows_of, LANES)

    for b in range(2 * blocks):
        for comp in range(comps):
            for half in range(parents // 8):
                incoming_ref[comp, 8 * half : 8 * half + 8, b * LANES : (b + 1) * LANES] = fields[
                    step, pl.ds(8 * half * rows_of + 2 * b + comp, 8, stride=rows_of), :
                ]

    def block(piece, index, weight, phase):
        field = fields.at[piece]
        shifted = []
        for half in range(2):
            cosine, sine = turn(phase[:, LANES * half : LANES * (half + 1)])
            shifted.append(shift_all(field, 2 * index + half, cosine, sine, parents, rows_of))
        shifted = split(jnp.concatenate(shifted, axis=1))
        both = contract(shifted, band(weight, picks), (1, 1))
        return both[:, :LANES], both[:, LANES:]

    def finish(index, main, before, after):
        columns = slice(LANES * index, LANES * (index + 1))
        value = main + jnp.where(lane < LANES // 2, before, after)
        out_ref[:, :, columns] = local_ref[:, :, columns] + value.reshape(comps, children, LANES)

    @pl.when(step == 0)
    def _():
        carried[0], carried[1] = block(0, 0, w_ref[:, : 2 * LANES], f_ref[:, : 2 * LANES])
        carried[2] = jnp.zeros((rows, LANES), jnp.float32)

    for b in range(1, blocks):
        columns = slice(2 * LANES * b, 2 * LANES * (b + 1))
        main, rim = block(step, b, w_ref[:, columns], f_ref[:, columns])
        finish(b - 1, carried[0], carried[2], rim)
        carried[2] = carried[1]
        carried[0] = main
        carried[1] = rim

    @pl.when(step < total - 1)
    def _():
        main, rim = block(step + 1, 0, wn_ref[...], fn_ref[...])
        finish(blocks - 1, carried[0], carried[2], rim)
        carried[2] = carried[1]
        carried[0] = main
        carried[1] = rim

    @pl.when(step == total - 1)
    def _():
        finish(blocks - 1, carried[0], carried[2], jnp.zeros((rows, LANES), jnp.float32))


def spread(me, child_local, weight, phase, sources):
    total = len(sources)
    parents, rows_of, _ = sources[0].shape
    comps, children, width = child_local.shape
    span = width // total
    blocks = span // LANES
    smem = pl.BlockSpec(memory_space=pltpu.SMEM)
    held = pl.BlockSpec((parents, rows_of, LANES), lambda g: (0, 0, 0))

    def after(g):
        return (0, jnp.minimum((g + 1) * blocks, total * blocks - 1))

    return pl.pallas_call(
        spread_kernel,
        grid=(total,),
        in_specs=[
            smem,
            pl.BlockSpec((comps, children, span), lambda g: (0, 0, g)),
            pl.BlockSpec((TAPS, 2 * span), lambda g: (0, g)),
            pl.BlockSpec((TAPS, 2 * LANES), after),
            pl.BlockSpec((CHILDREN, 2 * span), lambda g: (0, g)),
            pl.BlockSpec((CHILDREN, 2 * LANES), after),
        ]
        + [held] * total,
        out_specs=[
            pl.BlockSpec((comps, parents, 2 * span), lambda g: (0, 0, g)),
            pl.BlockSpec((comps, children, span), lambda g: (0, 0, g)),
        ],
        out_shape=[
            jax.ShapeDtypeStruct((comps, parents, 2 * width), jnp.float32),
            jax.ShapeDtypeStruct((comps, children, width), jnp.float32),
        ],
        scratch_shapes=[
            pltpu.VMEM((total, parents * rows_of, LANES), jnp.float32),
            pltpu.VMEM((3, comps * children, LANES), jnp.float32),
        ],
        name="spread",
        cost_estimate=pl.CostEstimate(flops=8 << 30, bytes_accessed=12 << 20, transcendentals=0),
    )(jnp.full((total,), me, jnp.int32), child_local, weight, weight, phase, phase, *sources)


def join_kernel(block_ref, from_left_ref, from_right_ref, out_ref):
    comps, children, _ = block_ref.shape
    step = pl.program_id(0)

    @pl.when(step == 0)
    def _():
        out_ref[...] = block_ref[...] + widen(from_left_ref[...], 0).reshape(comps, children, LANES)

    @pl.when(step == 1)
    def _():
        out_ref[...] = block_ref[...] + widen(from_right_ref[...], LANES - 8).reshape(comps, children, LANES)


def join(child_incoming, from_left, from_right):
    comps, children, width = child_incoming.shape
    end = width // LANES - 1
    edge = pl.BlockSpec((comps, children, LANES), lambda g: (0, 0, g * end))
    rim = pl.BlockSpec((8, comps * children), lambda g: (0, 0))
    return pl.pallas_call(
        join_kernel,
        grid=(2,),
        in_specs=[edge, rim, rim],
        out_specs=edge,
        out_shape=jax.ShapeDtypeStruct(child_incoming.shape, jnp.float32),
        input_output_aliases={0: 0},
        name="join",
        cost_estimate=pl.CostEstimate(flops=1 << 20, bytes_accessed=1 << 19, transcendentals=0),
    )(child_incoming, from_left, from_right)


def ring(count):
    forward = [(i, (i + 1) % count) for i in range(count)]
    return forward, [(target, source) for source, target in forward]


def fast(
    child_pattern,
    child_local,
    interp_weight,
    child_phase,
    translator,
    partners,
    operator_id,
    list_len,
):
    total = lax.axis_size("cluster")
    me = lax.axis_index("cluster")
    forward, backward = ring(lax.axis_size("sample"))
    first, last = rims(child_pattern)
    before = lax.ppermute(last, "sample", forward)
    after = lax.ppermute(first, "sample", backward)

    def swap(block, k):
        if k == 0:
            return block
        return lax.ppermute(block, "cluster", [(i, i ^ k) for i in range(total)])

    half = total // 2
    sent = [None] * total
    for base in (half, 0):
        made = aggregate(
            me, total, base, half, child_pattern, before, after, interp_weight, child_phase
        )
        for i in range(half):
            sent[base + i] = made[i]
    sources = [swap(sent[k], k) for k in range(total)]

    count, comps, samples = translator.shape
    table = translator.reshape(count, comps, samples // LANES, LANES).transpose(0, 2, 1, 3)
    table = table.reshape(count, comps * samples // LANES, LANES)
    rows = comps * samples // LANES // total
    table = lax.dynamic_slice_in_dim(table, me * rows, rows, 1)
    table = jnp.pad(table, ((0, 1), (0, 0), (0, 0)))
    slots = operator_id.shape[1]
    alive = jnp.arange(slots)[None, :] < list_len[:, None]
    operators = jnp.pad(jnp.where(alive, operator_id, count) * rows, ((0, UNROLL), (0, 0)))
    offsets = jnp.pad(partners * (2 * rows), ((0, UNROLL), (0, 0)))
    lengths = jnp.pad(list_len, (0, UNROLL))
    back = translate(
        me, offsets.reshape(-1), operators.reshape(-1), lengths, slots, table, sources
    )
    fields = [swap(back[k], k) for k in range(total)]
    low, high = outer(me, interp_weight, child_phase, fields)
    from_left = lax.ppermute(high, "sample", forward)
    from_right = lax.ppermute(low, "sample", backward)
    incoming, child_incoming = spread(me, child_local, interp_weight, child_phase, fields)
    return incoming, join(child_incoming, from_left, from_right)


def with_halo(block, sides, width):
    for axis, dim in sides:
        forward, backward = ring(lax.axis_size(axis))
        low = lax.ppermute(
            lax.slice_in_dim(block, block.shape[dim] - width, None, axis=dim), axis, forward
        )
        high = lax.ppermute(lax.slice_in_dim(block, 0, width, axis=dim), axis, backward)
        block = jnp.concatenate([low, block, high], axis=dim)
    return block


def translate_rows(pattern, table, partner_rows, operator_rows, lengths):
    receivers = partner_rows.shape[0]
    slot_count = partner_rows.shape[1]
    group_size = 16
    sample_count = pattern.shape[2]

    def advance(block, total):
        partner_cols = lax.dynamic_slice_in_dim(partner_rows, block * group_size, group_size, 1)
        operator_cols = lax.dynamic_slice_in_dim(operator_rows, block * group_size, group_size, 1)
        slot_index = block * group_size + jnp.arange(group_size)
        alive_mask = (slot_index[None, :] < lengths[:, None]).astype(jnp.float32)
        source = jnp.take(pattern, partner_cols, axis=1)
        coupling = jnp.take(table, operator_cols, axis=0)
        coup_real = coupling[:, :, 0] * alive_mask[:, :, None]
        coup_imag = coupling[:, :, 1] * alive_mask[:, :, None]
        real_part = jnp.sum(coup_real * source[0] - coup_imag * source[1], axis=1)
        imag_part = jnp.sum(coup_real * source[1] + coup_imag * source[0], axis=1)
        return total + jnp.stack([real_part, imag_part])

    start_total = jnp.zeros((2, receivers, sample_count), jnp.float32)
    return lax.fori_loop(0, slot_count // group_size, advance, start_total)


def phase_sum(upsampled, cosine, sine, parent_count):
    grouped = upsampled.reshape(2, parent_count, CHILDREN, upsampled.shape[2])
    real_part = jnp.sum(cosine[None] * grouped[0] - sine[None] * grouped[1], axis=1)
    imag_part = jnp.sum(cosine[None] * grouped[1] + sine[None] * grouped[0], axis=1)
    return jnp.stack([real_part, imag_part])


def phase_spread(incoming, cosine, sine):
    shifted_real = cosine[None] * incoming[0][:, None] + sine[None] * incoming[1][:, None]
    shifted_imag = cosine[None] * incoming[1][:, None] - sine[None] * incoming[0][:, None]
    return jnp.stack([shifted_real, shifted_imag]).reshape(2, -1, incoming.shape[2])


def plain(
    child_pattern,
    child_local,
    interp_weight,
    child_phase,
    translator,
    partners,
    operator_id,
    list_len,
):
    rim_width = TAPS // 2
    child_count = child_pattern.shape[1]
    parent_count = child_count // CHILDREN
    half_samples = child_pattern.shape[2]
    cosine = jnp.cos(child_phase)
    sine = jnp.sin(child_phase)
    cos_even = cosine[:, 0::2]
    cos_odd = cosine[:, 1::2]
    sin_even = sine[:, 0::2]
    sin_odd = sine[:, 1::2]
    weight_even = interp_weight[:, 0::2]
    weight_odd = interp_weight[:, 1::2]
    padded = with_halo(child_pattern, (("sample", 2),), rim_width)
    up_even = jnp.zeros((2, child_count, half_samples), jnp.float32)
    up_odd = jnp.zeros((2, child_count, half_samples), jnp.float32)
    for tap in range(TAPS):
        window = padded[:, :, 1 + tap : 1 + tap + half_samples]
        up_even = up_even + weight_even[tap][None, None, :] * window
        up_odd = up_odd + weight_odd[tap][None, None, :] * window
    parent_even = phase_sum(up_even, cos_even, sin_even, parent_count)
    parent_odd = phase_sum(up_odd, cos_odd, sin_odd, parent_count)
    parent = jnp.stack([parent_even, parent_odd], axis=3).reshape(2, parent_count, 2 * half_samples)
    cluster_index = lax.axis_index("cluster")
    whole = lax.all_gather(parent, "cluster", axis=1, tiled=True)
    first_row = cluster_index * parent_count
    own_partners = lax.dynamic_slice_in_dim(partners, first_row, parent_count, 0)
    own_operators = lax.dynamic_slice_in_dim(operator_id, first_row, parent_count, 0)
    own_lengths = lax.dynamic_slice_in_dim(list_len, first_row, parent_count, 0)
    incoming = translate_rows(whole, translator, own_partners, own_operators, own_lengths)
    shift_even = phase_spread(incoming[:, :, 0::2], cos_even, sin_even)
    shift_odd = phase_spread(incoming[:, :, 1::2], cos_odd, sin_odd)
    weighted = jnp.stack(
        [
            weight_even[tap][None, None, :] * shift_even
            + weight_odd[tap][None, None, :] * shift_odd
            for tap in range(TAPS)
        ]
    )
    padded_weighted = with_halo(weighted, (("sample", 3),), rim_width)
    child_incoming = child_local
    for tap in range(TAPS):
        offset = 2 * rim_width - 1 - tap
        child_incoming = child_incoming + padded_weighted[tap, :, :, offset : offset + half_samples]
    return (incoming, child_incoming)


def local(child_pattern, *rest):
    total = lax.axis_size("cluster")
    share = child_pattern.shape[2] // total
    fits = total & (total - 1) == 0 and share >= 2 * LANES and share % (2 * LANES) == 0
    fits = fits and share * total == child_pattern.shape[2]
    return (fast if fits else plain)(child_pattern, *rest)


def solution(mesh):
    placed = (
        P(None, "cluster", "sample"),
        P(None, "cluster", "sample"),
        P(None, "sample"),
        P(None, "sample"),
        P(None, None, "sample"),
        P(),
        P(),
        P(),
    )
    return jax.shard_map(
        local,
        mesh=mesh,
        in_specs=placed,
        out_specs=(P(None, "cluster", "sample"), P(None, "cluster", "sample")),
        check_vma=False,
    )
```

```python
import functools

import jax
import jax.numpy as jnp
from jax import lax
from jax.experimental import pallas as pl
from jax.experimental.pallas import tpu as pltpu
from jax.sharding import PartitionSpec as P


TAPS = 6
CHILDREN = 8
LANES = 128
RIM = TAPS // 2
GROUP = 4
UNROLL = 16
GRANT = pltpu.CompilerParams(vmem_limit_bytes=12 << 20)


def on_chip(*arrays):
    return [pltpu.with_memory_space_constraint(array, pltpu.VMEM) for array in arrays]


def split(values):
    high = values.astype(jnp.bfloat16)
    low = (values - high.astype(jnp.float32)).astype(jnp.bfloat16)
    return high, low


def contract(left, right, dims):
    (lh, ll), (rh, rl) = left, right
    axis_l, axis_r = dims
    return lax.dot_general(
        jnp.concatenate([lh, ll, lh], axis=axis_l),
        jnp.concatenate([rh, rh, rl], axis=axis_r),
        (((axis_l,), (axis_r,)), ((), ())),
        preferred_element_type=jnp.float32,
    )


def turn(phase):
    half = 0.5 * phase
    square = half * half
    sine = jnp.full_like(square, -1.0 / 39916800)
    for term in (1.0 / 362880, -1.0 / 5040, 1.0 / 120, -1.0 / 6, 1.0):
        sine = sine * square + term
    sine = sine * half
    cosine = jnp.full_like(square, 1.0 / 479001600)
    for term in (-1.0 / 3628800, 1.0 / 40320, -1.0 / 720, 1.0 / 24, -0.5, 1.0):
        cosine = cosine * square + term
    double = sine + sine
    return 1.0 - double * sine, double * cosine


def tap_rows():
    row = lax.broadcasted_iota(jnp.int32, (8, LANES), 0)
    half = lax.broadcasted_iota(jnp.int32, (8, LANES), 1) // 2
    near = row - half + (RIM - 1)
    picks = []
    for tile in range(-1, LANES // 16 + 1):
        tap = near + 8 * tile
        picks.append(jnp.where((tap >= 0) & (tap < TAPS), tap, TAPS))
    return picks


def band_tiles(weight, picks):
    padded = jnp.concatenate([weight, jnp.zeros((8 - TAPS, LANES), jnp.float32)], axis=0)
    return [
        jnp.take_along_axis(padded, pick, axis=0, mode="promise_in_bounds") for pick in picks
    ]


def band(weight, picks):
    high = weight.astype(jnp.bfloat16).astype(jnp.float32)
    parts = []
    zero = jnp.zeros((8, LANES), jnp.float32)
    inner = LANES // 16
    for piece in (high, weight - high):
        first = band_tiles(piece[:, :LANES], picks)
        second = band_tiles(piece[:, LANES:], picks)
        left = first[1:] + [zero] * (inner - 1) + [zero] * (2 * inner - 1) + [first[0]]
        right = [zero] * (inner - 1) + second[:-1] + [second[-1]] + [zero] * (2 * inner - 1)
        columns = [jnp.concatenate(tiles, axis=0).astype(jnp.bfloat16) for tiles in (left, right)]
        parts.append(jnp.concatenate(columns, axis=1))
    return tuple(parts)


def picker(first, rows):
    row = lax.broadcasted_iota(jnp.int32, (rows, LANES), 0)
    lane = lax.broadcasted_iota(jnp.int32, (rows, LANES), 1)
    return (lane == row + first).astype(jnp.bfloat16)


def merge(first, second, step, sub):
    low = (sub & step) == 0
    return jnp.where(low, first, second) + pltpu.roll(jnp.where(low, second, first), step, 0)


def sublane_sums(blocks, sub):
    for step in (1, 2, 4):
        blocks = [merge(blocks[i], blocks[i + 1], step, sub) for i in range(0, len(blocks), 2)]
    return blocks[0]


def exchange(to_right, to_left):
    forward, backward = ring(lax.axis_size("sample"))
    from_left = lax.ppermute(to_right, "sample", forward)
    from_right = lax.ppermute(to_left, "sample", backward)
    return from_left, from_right


def narrow(block, at):
    pick = picker(at, 8)
    high, low = split(block)
    return lax.dot_general(
        jnp.concatenate([pick, pick], axis=1),
        jnp.concatenate([high, low], axis=1),
        (((1,), (1,)), ((), ())),
        preferred_element_type=jnp.float32,
    )


def rim_kernel(first_ref, last_ref, right_ref, left_ref):
    rows = first_ref.shape[0] * first_ref.shape[1]
    right_ref[...] = narrow(last_ref[...].reshape(rows, LANES), LANES - 8)
    left_ref[...] = narrow(first_ref[...].reshape(rows, LANES), 0)


def rims(child):
    comps, children, width = child.shape
    rows = comps * children
    child = pltpu.with_memory_space_constraint(child, pltpu.HBM)
    return pl.pallas_call(
        rim_kernel,
        grid=(1,),
        in_specs=[
            pl.BlockSpec((comps, children, LANES), lambda g: (0, 0, 0)),
            pl.BlockSpec((comps, children, LANES), lambda g: (0, 0, width // LANES - 1)),
        ],
        out_specs=[pl.BlockSpec((8, rows), lambda g: (0, 0))] * 2,
        out_shape=[jax.ShapeDtypeStruct((8, rows), jnp.float32)] * 2,
        name="rims",
        compiler_params=GRANT,
        cost_estimate=pl.CostEstimate(flops=1 << 20, bytes_accessed=1 << 18, transcendentals=0),
    )(child, child)


def widen(compact, at):
    high, low = split(compact)
    pick = picker(at, 8)
    return lax.dot_general(
        jnp.concatenate([high, low], axis=0),
        jnp.concatenate([pick, pick], axis=0),
        (((0,), (0,)), ((), ())),
        preferred_element_type=jnp.float32,
    )


def aggregate_kernel(me_ref, ks_ref, x_ref, before_ref, after_ref, w_ref, f_ref, *rest):
    outs, (held, made_ref, even_ref, odd_ref, arrived) = rest[:-5], rest[-5:]
    comps, children, width = x_ref.shape
    rows = comps * children
    parents = children // CHILDREN
    total = me_ref.shape[0]
    count = len(outs)
    span = width // total
    quads = span // (2 * LANES)
    lane = lax.broadcasted_iota(jnp.int32, (rows, LANES), 1)
    inner = lane < LANES // 2
    sub = lax.broadcasted_iota(jnp.int32, (8, LANES), 0)
    picks = tap_rows()

    def copies(i):
        piece = me_ref[0] ^ ks_ref[i]
        left = jnp.maximum(piece * span - LANES, 0)
        right = jnp.minimum(piece * span + span, width - LANES)
        return [
            pltpu.make_async_copy(
                x_ref.at[:, :, pl.ds(pl.multiple_of(source, LANES), size)],
                held.at[i, :, :, target : target + size],
                arrived.at[i, j],
            )
            for j, (source, target, size) in enumerate(
                ((left, 0, LANES), (piece * span, LANES, span), (right, LANES + span, LANES))
            )
        ]

    for i in range(count):
        for copy in copies(i):
            copy.start()

    def lanes_of(i, at):
        return held[i, :, :, at * LANES : (at + 1) * LANES].reshape(rows, LANES)

    def raise_quad(piece, i, quad, up_ref):
        first = 2 * quad + 1
        sides = split(jnp.where(inner, lanes_of(i, first + 2), lanes_of(i, first - 1)))
        here = [split(lanes_of(i, first)), split(lanes_of(i, first + 1))]
        rims = [
            [jnp.where(inner, here[1][j], sides[j]) for j in range(2)],
            [jnp.where(inner, sides[j], here[0][j]) for j in range(2)],
        ]
        for b in range(2):
            left_hand = [jnp.concatenate([here[b][j], rims[b][j]], axis=1) for j in range(2)]
            at = pl.multiple_of((piece * quads + quad) * 4 * LANES + b * 2 * LANES, 2 * LANES)
            weight = w_ref[:, pl.ds(at, 2 * LANES)]
            up_ref[:, 2 * LANES * b : 2 * LANES * (b + 1)] = contract(left_hand, band(weight, picks), (1, 0))

    def sum_quad(piece, quad, slot, up_ref):
        at = pl.multiple_of((piece * quads + quad) * 4 * LANES, 4 * LANES)
        cosines, sines = turn(f_ref[:, pl.ds(at, 4 * LANES)])
        for p in range(parents):
            gathered = []
            for b in range(4):
                col = slice(LANES * b, LANES * (b + 1))
                cosine, sine = cosines[:, col], sines[:, col]
                real = up_ref[p * CHILDREN : (p + 1) * CHILDREN, col]
                imag = up_ref[(parents + p) * CHILDREN : (parents + p + 1) * CHILDREN, col]
                gathered.append(cosine * real - sine * imag)
                gathered.append(cosine * imag + sine * real)
            made_ref[slot, p, 8 * quad : 8 * quad + 8, :] = sublane_sums(gathered, sub)

    ups = (even_ref, odd_ref)

    def advance(i, carry):
        piece = me_ref[0] ^ ks_ref[i]
        earlier = jnp.maximum(i - 1, 0)
        former = me_ref[0] ^ ks_ref[earlier]
        for copy in copies(i):
            copy.wait()

        @pl.when(piece == 0)
        def _():
            held[i, :, :, :LANES] = widen(before_ref[...], LANES - 8).reshape(comps, children, LANES)

        @pl.when(piece == total - 1)
        def _():
            held[i, :, :, LANES + span :] = widen(after_ref[...], 0).reshape(comps, children, LANES)

        for quad in range(quads):
            raise_quad(piece, i, quad, ups[quad % 2])
            if quad:
                sum_quad(piece, quad - 1, i, ups[(quad - 1) % 2])
            else:
                sum_quad(former, quads - 1, earlier, ups[1])
        return carry

    odd_ref[...] = jnp.zeros_like(odd_ref)
    lax.fori_loop(0, count, advance, 0)
    sum_quad(me_ref[0] ^ ks_ref[count - 1], quads - 1, count - 1, ups[1])
    for i in range(count):
        outs[i][...] = made_ref[i]


def aggregate(me, total, ks, child, before, after, weight, phase):
    count = len(ks)
    comps, children, width = child.shape
    parents = children // CHILDREN
    rows = comps * children
    span = width // total
    rows_of = 4 * (span // LANES)
    smem = pl.BlockSpec(memory_space=pltpu.SMEM)
    vmem = pl.BlockSpec(memory_space=pltpu.VMEM)
    return pl.pallas_call(
        aggregate_kernel,
        in_specs=[smem] * 2 + [pl.BlockSpec(memory_space=pl.ANY)] + [vmem] * 4,
        out_specs=[vmem] * count,
        out_shape=[jax.ShapeDtypeStruct((parents, rows_of, LANES), jnp.float32)] * count,
        scratch_shapes=[
            pltpu.VMEM((count, comps, children, span + 2 * LANES), jnp.float32),
            pltpu.VMEM((count, parents, rows_of, LANES), jnp.float32),
            pltpu.VMEM((rows, 4 * LANES), jnp.float32),
            pltpu.VMEM((rows, 4 * LANES), jnp.float32),
            pltpu.SemaphoreType.DMA((count, 3)),
        ],
        name="aggregate",
        compiler_params=GRANT,
        cost_estimate=pl.CostEstimate(flops=4 << 30, bytes_accessed=6 << 20, transcendentals=0),
    )(
        jnp.full((total,), me, jnp.int32),
        jnp.array(ks, jnp.int32),
        pltpu.with_memory_space_constraint(child, pltpu.HBM),
        *on_chip(before, after, weight, phase),
    )


def place_kernel(me_ref, *rest):
    total = me_ref.shape[0]
    sources, held = rest[:total], rest[total]
    parents, rows, _ = sources[0].shape
    odd = (lax.broadcasted_iota(jnp.int32, (rows, LANES), 0) & 1) == 1
    for k in range(total):
        first = (me_ref[0] ^ k) * parents

        def place(p, carry, k=k, first=first):
            block = sources[k][p]
            at = pl.multiple_of((first + p) * 2 * rows, 2 * rows)
            held[pl.ds(at, rows), :] = block
            held[pl.ds(at + rows, rows), :] = jnp.where(
                odd, pltpu.roll(block, 1, 0), pltpu.roll(block, rows - 1, 0)
            )
            return carry

        lax.fori_loop(0, parents, place, 0, unroll=4)


def place(me, sources):
    total = len(sources)
    parents, rows, lanes = sources[0].shape
    vmem = pl.BlockSpec(memory_space=pltpu.VMEM)
    return pl.pallas_call(
        place_kernel,
        in_specs=[pl.BlockSpec(memory_space=pltpu.SMEM)] + [vmem] * total,
        out_specs=vmem,
        out_shape=jax.ShapeDtypeStruct((total * parents * 2 * rows, lanes), jnp.float32),
        name="place",
        compiler_params=GRANT,
        cost_estimate=pl.CostEstimate(flops=1 << 20, bytes_accessed=3 << 20, transcendentals=0),
    )(jnp.full((total,), me, jnp.int32), *on_chip(*sources))


def translate_kernel(base, me_ref, ends_ref, at_ref, into_ref, keep_ref, partner_ref, op_ref, table_ref, held, *rest):
    outs, sums = rest[:-1], rest[-1]
    count = len(outs)
    parents, rows, _ = outs[0].shape
    table = table_ref.reshape(table_ref.shape[0] * rows, LANES)
    odd = (lax.broadcasted_iota(jnp.int32, (rows, LANES), 0) & 1) == 1
    part = ((me_ref[0] ^ base) // count) * count * parents
    start = jnp.where(part > 0, ends_ref[jnp.maximum(part - 1, 0)], 0)
    stop = ends_ref[part + count * parents - 1]
    entries = at_ref.shape[0] - UNROLL + 1
    slots = op_ref.shape[0] - GROUP + 1

    def add(step, totals):
        for group in range(UNROLL):
            index = start + step * UNROLL
            at = at_ref.at[pl.ds(group, entries)][index]
            into = pl.multiple_of(into_ref.at[pl.ds(group, entries)][index], 2 * rows)
            keep = keep_ref.at[pl.ds(group, entries)][index]
            direct, crossed = [], []
            for u in range(GROUP):
                operator = table[pl.ds(pl.multiple_of(op_ref.at[pl.ds(u, slots)][at], rows), rows), :]
                partner = pl.multiple_of(partner_ref.at[pl.ds(u, slots)][at], 2 * rows)
                direct.append(operator * held[pl.ds(partner, rows), :])
                crossed.append(operator * held[pl.ds(partner + rows, rows), :])
            while len(direct) > 1:
                direct = [a + b for a, b in zip(direct[::2], direct[1::2])]
                crossed = [a + b for a, b in zip(crossed[::2], crossed[1::2])]
            totals = (totals[0] * keep + direct[0], totals[1] * keep + crossed[0])
            sums[pl.ds(into, rows), :] = totals[0]
            sums[pl.ds(into + rows, rows), :] = totals[1]
        return totals

    zero = jnp.zeros((rows, LANES), jnp.float32)
    lax.fori_loop(0, (stop - start + UNROLL - 1) // UNROLL, add, (zero, zero))
    for k in range(count):
        first = (me_ref[0] ^ (base + k)) * parents

        def combine(q, carry, out_ref=outs[k], first=first):
            at = pl.multiple_of((first + q) * 2 * rows, 2 * rows)
            direct, crossed = sums[pl.ds(at, rows), :], sums[pl.ds(at + rows, rows), :]
            real = direct - pltpu.roll(direct, rows - 1, 0)
            imag = crossed + pltpu.roll(crossed, 1, 0)
            out_ref[q] = jnp.where(odd, imag, real)
            return carry

        lax.fori_loop(0, parents, combine, 0, unroll=4)


def plan(partners, operators, lengths, count, rows):
    receivers, slots = operators.shape
    rounds = (lengths + GROUP - 1) // GROUP
    index = jnp.arange(receivers)
    ends = jnp.sum(jnp.where(index[None, :] <= index[:, None], rounds[None, :], 0), axis=1)
    group = jnp.arange(receivers * ((slots + GROUP - 1) // GROUP) + UNROLL)
    passed = ends[None, :] <= group[:, None]
    receiver = jnp.sum(passed.astype(jnp.int32), axis=1)
    slot = (group - jnp.max(jnp.where(passed, ends[None, :], 0), axis=1)) * GROUP
    alive = jnp.arange(slots)[None, :] < lengths[:, None]
    operators = jnp.pad(jnp.where(alive, operators, count) * rows, ((0, 1), (0, 0)), constant_values=count * rows)
    partners = jnp.pad(partners * (2 * rows), ((0, 1), (0, 0)))
    return (
        ends,
        receiver * slots + slot,
        receiver * (2 * rows),
        (slot > 0).astype(jnp.float32),
        partners.reshape(-1),
        operators.reshape(-1),
    )


def translate(me, total, base, count, lists, table, held):
    rows, lanes = table.shape[1:]
    parents = held.shape[0] // (2 * rows * total)
    smem = pl.BlockSpec(memory_space=pltpu.SMEM)
    vmem = pl.BlockSpec(memory_space=pltpu.VMEM)
    return pl.pallas_call(
        functools.partial(translate_kernel, base),
        in_specs=[smem] * (1 + len(lists)) + [vmem] * 2,
        out_specs=[vmem] * count,
        out_shape=[jax.ShapeDtypeStruct((parents, rows, lanes), jnp.float32)] * count,
        scratch_shapes=[pltpu.VMEM(((total * parents + 1) * 2 * rows, lanes), jnp.float32)],
        name="translate",
        compiler_params=GRANT,
        cost_estimate=pl.CostEstimate(flops=4 << 30, bytes_accessed=4 << 20, transcendentals=0),
    )(jnp.full((total,), me, jnp.int32), *lists, *on_chip(table, held))


def spread_kernel(me_ref, local_ref, w_ref, f_ref, *rest):
    total = me_ref.shape[0]
    sources = rest[:total]
    incoming_ref, out_ref, low_ref, high_ref, fields, even, odd, mains, rim_ref = rest[total:]
    stages = (even, odd)
    parents, rows_of, _ = sources[0].shape
    blocks = rows_of // 4
    comps, children, _ = out_ref.shape
    rows = comps * children
    step = pl.program_id(0)
    me = me_ref[0]
    lane = lax.broadcasted_iota(jnp.int32, (rows, LANES), 1)
    picks = tap_rows()
    end = total * blocks - 1

    def stage(index, b):
        index = jnp.minimum(index, end)
        piece = index // blocks
        target = stages[b % 2]
        at = pl.multiple_of(index * 2 * LANES, 2 * LANES)
        cosines, sines = turn(f_ref[:, pl.ds(at, 2 * LANES)])
        for half in range(2):
            column = slice(LANES * half, LANES * (half + 1))
            cosine, sine = cosines[:, column], sines[:, column]
            row = 4 * (b % blocks) + 2 * half
            for p in range(0, parents, 2):
                reals, imags = [], []
                for q in (p, p + 1):
                    real = jnp.broadcast_to(fields[piece, pl.ds(q * rows_of + row, 1), :], (CHILDREN, LANES))
                    imag = jnp.broadcast_to(fields[piece, pl.ds(q * rows_of + row + 1, 1), :], (CHILDREN, LANES))
                    reals.append(cosine * real + sine * imag)
                    imags.append(cosine * imag - sine * real)
                for comp, pair in enumerate((reals, imags)):
                    first = comp * children + p * CHILDREN
                    high, low = split(jnp.concatenate(pair, axis=0))
                    target[0, first : first + 2 * CHILDREN, column] = high
                    target[1, first : first + 2 * CHILDREN, column] = low

    def multiply(index, b):
        at = pl.multiple_of(jnp.minimum(index, end) * 2 * LANES, 2 * LANES)
        weight = w_ref[:, pl.ds(at, 2 * LANES)]
        source = stages[b % 2]
        both = contract((source[0], source[1]), band(weight, picks), (1, 1))
        mains[b % 2] = both[:, :LANES]
        rim_ref[b % 4] = both[:, LANES:]

    @pl.when(step == 0)
    def _():
        for k in range(total):
            fields[me ^ k] = sources[k][...].reshape(parents * rows_of, LANES)
        stage(jnp.int32(0), 0)
        multiply(jnp.int32(0), 0)
        stage(jnp.int32(1), 1)
        rim_ref[3] = jnp.zeros((rows, LANES), jnp.float32)
        low_ref[...] = narrow(rim_ref[0], LANES - 8)

    inside = jnp.where(step < total - 1, 1.0, 0.0).astype(jnp.float32)
    first = step * blocks
    for b in range(1, blocks + 1):
        multiply(first + b, b)
        stage(first + b + 1, b + 1)
        columns = slice(LANES * (b - 1), LANES * b)
        after = rim_ref[b % 4] * inside if b == blocks else rim_ref[b % 4]
        value = mains[(b - 1) % 2] + jnp.where(lane < LANES // 2, rim_ref[(b - 2) % 4], after)
        lanes = pl.ds(pl.multiple_of((first + b - 1) * LANES, LANES), LANES)
        out_ref[:, :, columns] = local_ref[:, :, lanes] + value.reshape(comps, children, LANES)

    for b in range(2 * blocks):
        for comp in range(comps):
            for part in range(parents // 8):
                incoming_ref[comp, 8 * part : 8 * part + 8, b * LANES : (b + 1) * LANES] = fields[
                    step, pl.ds(8 * part * rows_of + 2 * b + comp, 8, stride=rows_of), :
                ]

    @pl.when(step == total - 1)
    def _():
        high_ref[...] = narrow(rim_ref[(blocks - 1) % 4], 0)


def spread(me, child_local, weight, phase, sources):
    total = len(sources)
    parents, rows_of, _ = sources[0].shape
    comps, children, width = child_local.shape
    rows = comps * children
    span = width // total
    smem = pl.BlockSpec(memory_space=pltpu.SMEM)
    vmem = pl.BlockSpec(memory_space=pltpu.VMEM)
    rim = pl.BlockSpec((8, rows), lambda g: (0, 0))
    return pl.pallas_call(
        spread_kernel,
        grid=(total,),
        in_specs=[smem] + [vmem] * (3 + total),
        out_specs=[
            pl.BlockSpec((comps, parents, 2 * span), lambda g: (0, 0, g)),
            pl.BlockSpec((comps, children, span), lambda g: (0, 0, g)),
            rim,
            rim,
        ],
        out_shape=[
            jax.ShapeDtypeStruct((comps, parents, 2 * width), jnp.float32),
            jax.ShapeDtypeStruct((comps, children, width), jnp.float32),
            jax.ShapeDtypeStruct((8, rows), jnp.float32),
            jax.ShapeDtypeStruct((8, rows), jnp.float32),
        ],
        scratch_shapes=[
            pltpu.VMEM((total, parents * rows_of, LANES), jnp.float32),
            pltpu.VMEM((2, rows, 2 * LANES), jnp.bfloat16),
            pltpu.VMEM((2, rows, 2 * LANES), jnp.bfloat16),
            pltpu.VMEM((2, rows, LANES), jnp.float32),
            pltpu.VMEM((4, rows, LANES), jnp.float32),
        ],
        name="spread",
        compiler_params=GRANT,
        cost_estimate=pl.CostEstimate(flops=8 << 30, bytes_accessed=12 << 20, transcendentals=0),
    )(jnp.full((total,), me, jnp.int32), *on_chip(child_local, weight, phase, *sources))


def join_kernel(from_left_ref, from_right_ref, whole_ref, out_ref, held, arrived, left):
    del whole_ref
    comps, children, width = out_ref.shape
    ends = (0, width - LANES)
    reads = [
        pltpu.make_async_copy(out_ref.at[:, :, at : at + LANES], held.at[i], arrived.at[i])
        for i, at in enumerate(ends)
    ]
    writes = [
        pltpu.make_async_copy(held.at[i], out_ref.at[:, :, at : at + LANES], left.at[i])
        for i, at in enumerate(ends)
    ]
    for read in reads:
        read.start()
    for i, (rim_ref, at) in enumerate(((from_left_ref, 0), (from_right_ref, LANES - 8))):
        added = widen(rim_ref[...], at).reshape(comps, children, LANES)
        reads[i].wait()
        held[i] = held[i] + added
        writes[i].start()
    for write in writes:
        write.wait()


def join(child_incoming, from_left, from_right):
    comps, children, _ = child_incoming.shape
    whole = pl.BlockSpec(memory_space=pl.ANY)
    return pl.pallas_call(
        join_kernel,
        in_specs=[pl.BlockSpec(memory_space=pltpu.VMEM)] * 2 + [whole],
        out_specs=whole,
        out_shape=jax.ShapeDtypeStruct(child_incoming.shape, jnp.float32),
        input_output_aliases={2: 0},
        scratch_shapes=[
            pltpu.VMEM((2, comps, children, LANES), jnp.float32),
            pltpu.SemaphoreType.DMA((2,)),
            pltpu.SemaphoreType.DMA((2,)),
        ],
        name="join",
        compiler_params=GRANT,
        cost_estimate=pl.CostEstimate(flops=1 << 20, bytes_accessed=1 << 19, transcendentals=0),
    )(*on_chip(from_left, from_right), child_incoming)


def ring(count):
    forward = [(i, (i + 1) % count) for i in range(count)]
    return forward, [(target, source) for source, target in forward]


def fast(
    child_pattern,
    child_local,
    interp_weight,
    child_phase,
    translator,
    partners,
    operator_id,
    list_len,
):
    total = lax.axis_size("cluster")
    me = lax.axis_index("cluster")
    before, after = exchange(*rims(child_pattern))

    def swap(block, k):
        if k == 0:
            return block
        return lax.ppermute(block, "cluster", [(i, i ^ k) for i in range(total)])

    sent = [None] * total
    for ks in gathers(total):
        made = aggregate(me, total, ks, child_pattern, before, after, interp_weight, child_phase)
        for k, block in zip(ks, made):
            sent[k] = block
    sources = [swap(sent[k], k) for k in range(total)]

    translator, partners, operator_id, list_len, _ = lax.optimization_barrier(
        (translator, partners, operator_id, list_len, sent[0])
    )
    count, comps, samples = translator.shape
    table = translator.reshape(count, comps, samples // LANES, LANES).transpose(0, 2, 1, 3)
    table = table.reshape(count, comps * samples // LANES, LANES)
    rows = comps * samples // LANES // total
    table = lax.dynamic_slice_in_dim(table, me * rows, rows, 1)
    table = jnp.pad(table, ((0, 1), (0, 0), (0, 0)))
    lists = plan(partners, operator_id, list_len, count, rows)
    held = place(me, sources)
    back = translate(me, total, 0, total, lists, table, held)
    fields = [swap(back[k], k) for k in range(total)]
    incoming, child_incoming, low, high = spread(
        me, child_local, interp_weight, child_phase, fields
    )
    from_left, from_right = exchange(high, low)
    return incoming, join(child_incoming, from_left, from_right)


def gathers(total):
    if total == 8:
        return (7, 6, 5, 3), (2, 4, 1, 0)
    order = tuple(range(total - 1, -1, -1))
    return (order[: total // 2], order[total // 2 :])


def with_halo(block, sides, width):
    for axis, dim in sides:
        forward, backward = ring(lax.axis_size(axis))
        low = lax.ppermute(
            lax.slice_in_dim(block, block.shape[dim] - width, None, axis=dim), axis, forward
        )
        high = lax.ppermute(lax.slice_in_dim(block, 0, width, axis=dim), axis, backward)
        block = jnp.concatenate([low, block, high], axis=dim)
    return block


def translate_rows(pattern, table, partner_rows, operator_rows, lengths):
    receivers = partner_rows.shape[0]
    slot_count = partner_rows.shape[1]
    group_size = 16
    sample_count = pattern.shape[2]

    def advance(block, total):
        partner_cols = lax.dynamic_slice_in_dim(partner_rows, block * group_size, group_size, 1)
        operator_cols = lax.dynamic_slice_in_dim(operator_rows, block * group_size, group_size, 1)
        slot_index = block * group_size + jnp.arange(group_size)
        alive_mask = (slot_index[None, :] < lengths[:, None]).astype(jnp.float32)
        source = jnp.take(pattern, partner_cols, axis=1)
        coupling = jnp.take(table, operator_cols, axis=0)
        coup_real = coupling[:, :, 0] * alive_mask[:, :, None]
        coup_imag = coupling[:, :, 1] * alive_mask[:, :, None]
        real_part = jnp.sum(coup_real * source[0] - coup_imag * source[1], axis=1)
        imag_part = jnp.sum(coup_real * source[1] + coup_imag * source[0], axis=1)
        return total + jnp.stack([real_part, imag_part])

    start_total = jnp.zeros((2, receivers, sample_count), jnp.float32)
    return lax.fori_loop(0, slot_count // group_size, advance, start_total)


def phase_sum(upsampled, cosine, sine, parent_count):
    grouped = upsampled.reshape(2, parent_count, CHILDREN, upsampled.shape[2])
    real_part = jnp.sum(cosine[None] * grouped[0] - sine[None] * grouped[1], axis=1)
    imag_part = jnp.sum(cosine[None] * grouped[1] + sine[None] * grouped[0], axis=1)
    return jnp.stack([real_part, imag_part])


def phase_spread(incoming, cosine, sine):
    shifted_real = cosine[None] * incoming[0][:, None] + sine[None] * incoming[1][:, None]
    shifted_imag = cosine[None] * incoming[1][:, None] - sine[None] * incoming[0][:, None]
    return jnp.stack([shifted_real, shifted_imag]).reshape(2, -1, incoming.shape[2])


def plain(
    child_pattern,
    child_local,
    interp_weight,
    child_phase,
    translator,
    partners,
    operator_id,
    list_len,
):
    rim_width = TAPS // 2
    child_count = child_pattern.shape[1]
    parent_count = child_count // CHILDREN
    half_samples = child_pattern.shape[2]
    cosine = jnp.cos(child_phase)
    sine = jnp.sin(child_phase)
    cos_even = cosine[:, 0::2]
    cos_odd = cosine[:, 1::2]
    sin_even = sine[:, 0::2]
    sin_odd = sine[:, 1::2]
    weight_even = interp_weight[:, 0::2]
    weight_odd = interp_weight[:, 1::2]
    padded = with_halo(child_pattern, (("sample", 2),), rim_width)
    up_even = jnp.zeros((2, child_count, half_samples), jnp.float32)
    up_odd = jnp.zeros((2, child_count, half_samples), jnp.float32)
    for tap in range(TAPS):
        window = padded[:, :, 1 + tap : 1 + tap + half_samples]
        up_even = up_even + weight_even[tap][None, None, :] * window
        up_odd = up_odd + weight_odd[tap][None, None, :] * window
    parent_even = phase_sum(up_even, cos_even, sin_even, parent_count)
    parent_odd = phase_sum(up_odd, cos_odd, sin_odd, parent_count)
    parent = jnp.stack([parent_even, parent_odd], axis=3).reshape(2, parent_count, 2 * half_samples)
    cluster_index = lax.axis_index("cluster")
    whole = lax.all_gather(parent, "cluster", axis=1, tiled=True)
    first_row = cluster_index * parent_count
    own_partners = lax.dynamic_slice_in_dim(partners, first_row, parent_count, 0)
    own_operators = lax.dynamic_slice_in_dim(operator_id, first_row, parent_count, 0)
    own_lengths = lax.dynamic_slice_in_dim(list_len, first_row, parent_count, 0)
    incoming = translate_rows(whole, translator, own_partners, own_operators, own_lengths)
    shift_even = phase_spread(incoming[:, :, 0::2], cos_even, sin_even)
    shift_odd = phase_spread(incoming[:, :, 1::2], cos_odd, sin_odd)
    weighted = jnp.stack(
        [
            weight_even[tap][None, None, :] * shift_even
            + weight_odd[tap][None, None, :] * shift_odd
            for tap in range(TAPS)
        ]
    )
    padded_weighted = with_halo(weighted, (("sample", 3),), rim_width)
    child_incoming = child_local
    for tap in range(TAPS):
        offset = 2 * rim_width - 1 - tap
        child_incoming = child_incoming + padded_weighted[tap, :, :, offset : offset + half_samples]
    return (incoming, child_incoming)


def fits(width, total):
    share = width // total
    even = total > 1 and total & (total - 1) == 0 and share * total == width
    return even and share >= 4 * LANES and share % (4 * LANES) == 0


def local(child_pattern, *rest):
    if fits(child_pattern.shape[2], lax.axis_size("cluster")):
        return fast(child_pattern, *rest)
    return plain(child_pattern, *rest)


def solution(mesh):
    placed = (
        P(None, "cluster", "sample"),
        P(None, "cluster", "sample"),
        P(None, "sample"),
        P(None, "sample"),
        P(None, None, "sample"),
        P(),
        P(),
        P(),
    )
    return jax.shard_map(
        local,
        mesh=mesh,
        in_specs=placed,
        out_specs=(P(None, "cluster", "sample"), P(None, "cluster", "sample")),
        check_vma=False,
    )
```

```python
import jax
import jax.numpy as jnp
from jax import lax
from jax.experimental import pallas as pl
from jax.experimental.pallas import tpu as pltpu
from jax.sharding import PartitionSpec as P


TAPS = 6
CHILDREN = 8
LANES = 128
RIM = TAPS // 2
GROUP = 4
UNROLL = 16
GRANT = pltpu.CompilerParams(vmem_limit_bytes=12 << 20)


def on_chip(*arrays):
    return [pltpu.with_memory_space_constraint(array, pltpu.VMEM) for array in arrays]


def split(values):
    high = values.astype(jnp.bfloat16)
    low = (values - high.astype(jnp.float32)).astype(jnp.bfloat16)
    return high, low


def contract(left, right, dims):
    (lh, ll), (rh, rl) = left, right
    axis_l, axis_r = dims
    return lax.dot_general(
        jnp.concatenate([lh, ll, lh], axis=axis_l),
        jnp.concatenate([rh, rh, rl], axis=axis_r),
        (((axis_l,), (axis_r,)), ((), ())),
        preferred_element_type=jnp.float32,
    )


def turn(phase):
    half = 0.5 * phase
    square = half * half
    sine = jnp.full_like(square, -1.0 / 39916800)
    for term in (1.0 / 362880, -1.0 / 5040, 1.0 / 120, -1.0 / 6, 1.0):
        sine = sine * square + term
    sine = sine * half
    cosine = jnp.full_like(square, 1.0 / 479001600)
    for term in (-1.0 / 3628800, 1.0 / 40320, -1.0 / 720, 1.0 / 24, -0.5, 1.0):
        cosine = cosine * square + term
    double = sine + sine
    return 1.0 - double * sine, double * cosine


def tap_rows():
    row = lax.broadcasted_iota(jnp.int32, (8, LANES), 0)
    half = lax.broadcasted_iota(jnp.int32, (8, LANES), 1) // 2
    near = row - half + (RIM - 1)
    picks = []
    for tile in range(-1, LANES // 16 + 1):
        tap = near + 8 * tile
        picks.append(jnp.where((tap >= 0) & (tap < TAPS), tap, TAPS))
    return picks


def band_tiles(weight, picks):
    padded = jnp.concatenate([weight, jnp.zeros((8 - TAPS, LANES), jnp.float32)], axis=0)
    return [
        jnp.take_along_axis(padded, pick, axis=0, mode="promise_in_bounds") for pick in picks
    ]


def band(weight, picks):
    high = weight.astype(jnp.bfloat16).astype(jnp.float32)
    parts = []
    zero = jnp.zeros((8, LANES), jnp.float32)
    inner = LANES // 16
    for piece in (high, weight - high):
        first = band_tiles(piece[:, :LANES], picks)
        second = band_tiles(piece[:, LANES:], picks)
        left = first[1:] + [zero] * (inner - 1) + [zero] * (2 * inner - 1) + [first[0]]
        right = [zero] * (inner - 1) + second[:-1] + [second[-1]] + [zero] * (2 * inner - 1)
        columns = [jnp.concatenate(tiles, axis=0).astype(jnp.bfloat16) for tiles in (left, right)]
        parts.append(jnp.concatenate(columns, axis=1))
    return tuple(parts)


def picker(first, rows):
    row = lax.broadcasted_iota(jnp.int32, (rows, LANES), 0)
    lane = lax.broadcasted_iota(jnp.int32, (rows, LANES), 1)
    return (lane == row + first).astype(jnp.bfloat16)


def merge(first, second, step, sub):
    low = (sub & step) == 0
    return jnp.where(low, first, second) + pltpu.roll(jnp.where(low, second, first), step, 0)


def sublane_sums(blocks, sub):
    for step in (1, 2, 4):
        blocks = [merge(blocks[i], blocks[i + 1], step, sub) for i in range(0, len(blocks), 2)]
    return blocks[0]


def exchange(to_right, to_left):
    forward, backward = ring(lax.axis_size("sample"))
    from_left = lax.ppermute(to_right, "sample", forward)
    from_right = lax.ppermute(to_left, "sample", backward)
    return from_left, from_right


def narrow(block, at):
    pick = picker(at, 8)
    high, low = split(block)
    return lax.dot_general(
        jnp.concatenate([pick, pick], axis=1),
        jnp.concatenate([high, low], axis=1),
        (((1,), (1,)), ((), ())),
        preferred_element_type=jnp.float32,
    )


def rim_kernel(first_ref, last_ref, right_ref, left_ref):
    rows = first_ref.shape[0] * first_ref.shape[1]
    right_ref[...] = narrow(last_ref[...].reshape(rows, LANES), LANES - 8)
    left_ref[...] = narrow(first_ref[...].reshape(rows, LANES), 0)


def rims(child):
    comps, children, width = child.shape
    rows = comps * children
    child = pltpu.with_memory_space_constraint(child, pltpu.HBM)
    return pl.pallas_call(
        rim_kernel,
        grid=(1,),
        in_specs=[
            pl.BlockSpec((comps, children, LANES), lambda g: (0, 0, 0)),
            pl.BlockSpec((comps, children, LANES), lambda g: (0, 0, width // LANES - 1)),
        ],
        out_specs=[pl.BlockSpec((8, rows), lambda g: (0, 0))] * 2,
        out_shape=[jax.ShapeDtypeStruct((8, rows), jnp.float32)] * 2,
        name="rims",
        compiler_params=GRANT,
        cost_estimate=pl.CostEstimate(flops=1 << 20, bytes_accessed=1 << 18, transcendentals=0),
    )(child, child)


def widen(compact, at):
    high, low = split(compact)
    pick = picker(at, 8)
    return lax.dot_general(
        jnp.concatenate([high, low], axis=0),
        jnp.concatenate([pick, pick], axis=0),
        (((0,), (0,)), ((), ())),
        preferred_element_type=jnp.float32,
    )


def aggregate_kernel(me_ref, ks_ref, x_ref, before_ref, after_ref, w_ref, f_ref, *rest):
    outs, (held, made_ref, even_ref, odd_ref, arrived) = rest[:-5], rest[-5:]
    comps, children, width = x_ref.shape
    rows = comps * children
    parents = children // CHILDREN
    total = me_ref.shape[0]
    count = len(outs)
    span = width // total
    quads = span // (2 * LANES)
    lane = lax.broadcasted_iota(jnp.int32, (rows, LANES), 1)
    inner = lane < LANES // 2
    sub = lax.broadcasted_iota(jnp.int32, (8, LANES), 0)
    picks = tap_rows()

    def copies(i):
        piece = me_ref[0] ^ ks_ref[i]
        left = jnp.maximum(piece * span - LANES, 0)
        right = jnp.minimum(piece * span + span, width - LANES)
        return [
            pltpu.make_async_copy(
                x_ref.at[:, :, pl.ds(pl.multiple_of(source, LANES), size)],
                held.at[i, :, :, target : target + size],
                arrived.at[i, j],
            )
            for j, (source, target, size) in enumerate(
                ((left, 0, LANES), (piece * span, LANES, span), (right, LANES + span, LANES))
            )
        ]

    for i in range(count):
        for copy in copies(i):
            copy.start()

    def lanes_of(i, at):
        return held[i, :, :, at * LANES : (at + 1) * LANES].reshape(rows, LANES)

    def raise_quad(piece, i, quad, up_ref):
        first = 2 * quad + 1
        sides = split(jnp.where(inner, lanes_of(i, first + 2), lanes_of(i, first - 1)))
        here = [split(lanes_of(i, first)), split(lanes_of(i, first + 1))]
        rims = [
            [jnp.where(inner, here[1][j], sides[j]) for j in range(2)],
            [jnp.where(inner, sides[j], here[0][j]) for j in range(2)],
        ]
        for b in range(2):
            left_hand = [jnp.concatenate([here[b][j], rims[b][j]], axis=1) for j in range(2)]
            at = pl.multiple_of((piece * quads + quad) * 4 * LANES + b * 2 * LANES, 2 * LANES)
            weight = w_ref[:, pl.ds(at, 2 * LANES)]
            up_ref[:, 2 * LANES * b : 2 * LANES * (b + 1)] = contract(left_hand, band(weight, picks), (1, 0))

    def sum_quad(piece, quad, slot, up_ref):
        at = pl.multiple_of((piece * quads + quad) * 4 * LANES, 4 * LANES)
        cosines, sines = turn(f_ref[:, pl.ds(at, 4 * LANES)])
        for p in range(parents):
            gathered = []
            for b in range(4):
                col = slice(LANES * b, LANES * (b + 1))
                cosine, sine = cosines[:, col], sines[:, col]
                real = up_ref[p * CHILDREN : (p + 1) * CHILDREN, col]
                imag = up_ref[(parents + p) * CHILDREN : (parents + p + 1) * CHILDREN, col]
                gathered.append(cosine * real - sine * imag)
                gathered.append(cosine * imag + sine * real)
            made_ref[slot, p, 8 * quad : 8 * quad + 8, :] = sublane_sums(gathered, sub)

    ups = (even_ref, odd_ref)

    def advance(i, carry):
        piece = me_ref[0] ^ ks_ref[i]
        earlier = jnp.maximum(i - 1, 0)
        former = me_ref[0] ^ ks_ref[earlier]
        for copy in copies(i):
            copy.wait()

        @pl.when(piece == 0)
        def _():
            held[i, :, :, :LANES] = widen(before_ref[...], LANES - 8).reshape(comps, children, LANES)

        @pl.when(piece == total - 1)
        def _():
            held[i, :, :, LANES + span :] = widen(after_ref[...], 0).reshape(comps, children, LANES)

        for quad in range(quads):
            raise_quad(piece, i, quad, ups[quad % 2])
            if quad:
                sum_quad(piece, quad - 1, i, ups[(quad - 1) % 2])
            else:
                sum_quad(former, quads - 1, earlier, ups[1])
        return carry

    odd_ref[...] = jnp.zeros_like(odd_ref)
    lax.fori_loop(0, count, advance, 0)
    sum_quad(me_ref[0] ^ ks_ref[count - 1], quads - 1, count - 1, ups[1])
    for i in range(count):
        outs[i][...] = made_ref[i]


def aggregate(me, total, ks, child, before, after, weight, phase):
    count = len(ks)
    comps, children, width = child.shape
    parents = children // CHILDREN
    rows = comps * children
    span = width // total
    rows_of = 4 * (span // LANES)
    smem = pl.BlockSpec(memory_space=pltpu.SMEM)
    vmem = pl.BlockSpec(memory_space=pltpu.VMEM)
    return pl.pallas_call(
        aggregate_kernel,
        in_specs=[smem] * 2 + [pl.BlockSpec(memory_space=pl.ANY)] + [vmem] * 4,
        out_specs=[vmem] * count,
        out_shape=[jax.ShapeDtypeStruct((parents, rows_of, LANES), jnp.float32)] * count,
        scratch_shapes=[
            pltpu.VMEM((count, comps, children, span + 2 * LANES), jnp.float32),
            pltpu.VMEM((count, parents, rows_of, LANES), jnp.float32),
            pltpu.VMEM((rows, 4 * LANES), jnp.float32),
            pltpu.VMEM((rows, 4 * LANES), jnp.float32),
            pltpu.SemaphoreType.DMA((count, 3)),
        ],
        name="aggregate",
        compiler_params=GRANT,
        cost_estimate=pl.CostEstimate(flops=4 << 30, bytes_accessed=6 << 20, transcendentals=0),
    )(
        jnp.full((total,), me, jnp.int32),
        jnp.array(ks, jnp.int32),
        pltpu.with_memory_space_constraint(child, pltpu.HBM),
        *on_chip(before, after, weight, phase),
    )


def translate_kernel(me_ref, ends_ref, at_ref, into_ref, keep_ref, partner_ref, op_ref, table_ref, *rest):
    total = me_ref.shape[0]
    sources, outs, (held, sums) = rest[:total], rest[total:-2], rest[-2:]
    parents, rows, _ = outs[0].shape
    table = table_ref.reshape(table_ref.shape[0] * rows, LANES)
    odd = (lax.broadcasted_iota(jnp.int32, (rows, LANES), 0) & 1) == 1
    for k in range(total):
        first = (me_ref[0] ^ k) * parents

        def place(p, carry, k=k, first=first):
            block = sources[k][p]
            at = pl.multiple_of((first + p) * 2 * rows, 2 * rows)
            held[pl.ds(at, rows), :] = block
            held[pl.ds(at + rows, rows), :] = jnp.where(
                odd, pltpu.roll(block, 1, 0), pltpu.roll(block, rows - 1, 0)
            )
            return carry

        lax.fori_loop(0, parents, place, 0, unroll=4)

    entries = at_ref.shape[0] - UNROLL + 1
    slots = op_ref.shape[0] - GROUP + 1

    def add(step, totals):
        for group in range(UNROLL):
            index = step * UNROLL
            at = at_ref.at[pl.ds(group, entries)][index]
            into = pl.multiple_of(into_ref.at[pl.ds(group, entries)][index], 2 * rows)
            keep = keep_ref.at[pl.ds(group, entries)][index]
            direct, crossed = [], []
            for u in range(GROUP):
                operator = table[pl.ds(pl.multiple_of(op_ref.at[pl.ds(u, slots)][at], rows), rows), :]
                partner = pl.multiple_of(partner_ref.at[pl.ds(u, slots)][at], 2 * rows)
                direct.append(operator * held[pl.ds(partner, rows), :])
                crossed.append(operator * held[pl.ds(partner + rows, rows), :])
            while len(direct) > 1:
                direct = [a + b for a, b in zip(direct[::2], direct[1::2])]
                crossed = [a + b for a, b in zip(crossed[::2], crossed[1::2])]
            totals = (totals[0] * keep + direct[0], totals[1] * keep + crossed[0])
            sums[pl.ds(into, rows), :] = totals[0]
            sums[pl.ds(into + rows, rows), :] = totals[1]
        return totals

    zero = jnp.zeros((rows, LANES), jnp.float32)
    groups = ends_ref[ends_ref.shape[0] - 1]
    lax.fori_loop(0, (groups + UNROLL - 1) // UNROLL, add, (zero, zero))
    for k in range(total):
        first = (me_ref[0] ^ k) * parents

        def combine(q, carry, out_ref=outs[k], first=first):
            at = pl.multiple_of((first + q) * 2 * rows, 2 * rows)
            direct, crossed = sums[pl.ds(at, rows), :], sums[pl.ds(at + rows, rows), :]
            real = direct - pltpu.roll(direct, rows - 1, 0)
            imag = crossed + pltpu.roll(crossed, 1, 0)
            out_ref[q] = jnp.where(odd, imag, real)
            return carry

        lax.fori_loop(0, parents, combine, 0, unroll=4)


def plan(partners, operators, lengths, count, rows):
    receivers, slots = operators.shape
    rounds = (lengths + GROUP - 1) // GROUP
    index = jnp.arange(receivers)
    ends = jnp.sum(jnp.where(index[None, :] <= index[:, None], rounds[None, :], 0), axis=1)
    group = jnp.arange(receivers * ((slots + GROUP - 1) // GROUP) + UNROLL)
    passed = ends[None, :] <= group[:, None]
    receiver = jnp.sum(passed.astype(jnp.int32), axis=1)
    slot = (group - jnp.max(jnp.where(passed, ends[None, :], 0), axis=1)) * GROUP
    alive = jnp.arange(slots)[None, :] < lengths[:, None]
    operators = jnp.pad(jnp.where(alive, operators, count) * rows, ((0, 1), (0, 0)), constant_values=count * rows)
    partners = jnp.pad(partners * (2 * rows), ((0, 1), (0, 0)))
    return (
        ends,
        receiver * slots + slot,
        receiver * (2 * rows),
        (slot > 0).astype(jnp.float32),
        partners.reshape(-1),
        operators.reshape(-1),
    )


def translate(me, lists, table, sources):
    total = len(sources)
    parents, rows, lanes = sources[0].shape
    smem = pl.BlockSpec(memory_space=pltpu.SMEM)
    vmem = pl.BlockSpec(memory_space=pltpu.VMEM)
    return pl.pallas_call(
        translate_kernel,
        in_specs=[smem] * (1 + len(lists)) + [vmem] * (1 + total),
        out_specs=[vmem] * total,
        out_shape=[jax.ShapeDtypeStruct((parents, rows, lanes), jnp.float32)] * total,
        scratch_shapes=[
            pltpu.VMEM((total * parents * 2 * rows, lanes), jnp.float32),
            pltpu.VMEM(((total * parents + 1) * 2 * rows, lanes), jnp.float32),
        ],
        name="translate",
        compiler_params=GRANT,
        cost_estimate=pl.CostEstimate(flops=4 << 30, bytes_accessed=4 << 20, transcendentals=0),
    )(jnp.full((total,), me, jnp.int32), *lists, *on_chip(table, *sources))


def spread_kernel(me_ref, local_ref, w_ref, f_ref, *rest):
    total = me_ref.shape[0]
    sources = rest[:total]
    incoming_ref, out_ref, low_ref, high_ref, fields, even, odd, mains, rim_ref = rest[total:]
    stages = (even, odd)
    parents, rows_of, _ = sources[0].shape
    blocks = rows_of // 4
    comps, children, _ = out_ref.shape
    rows = comps * children
    step = pl.program_id(0)
    me = me_ref[0]
    lane = lax.broadcasted_iota(jnp.int32, (rows, LANES), 1)
    picks = tap_rows()
    end = total * blocks - 1

    def stage(index, b):
        index = jnp.minimum(index, end)
        piece = index // blocks
        target = stages[b % 2]
        at = pl.multiple_of(index * 2 * LANES, 2 * LANES)
        cosines, sines = turn(f_ref[:, pl.ds(at, 2 * LANES)])
        for half in range(2):
            column = slice(LANES * half, LANES * (half + 1))
            cosine, sine = cosines[:, column], sines[:, column]
            row = 4 * (b % blocks) + 2 * half
            for p in range(parents):
                real = jnp.broadcast_to(fields[piece, pl.ds(p * rows_of + row, 1), :], (CHILDREN, LANES))
                imag = jnp.broadcast_to(fields[piece, pl.ds(p * rows_of + row + 1, 1), :], (CHILDREN, LANES))
                first = p * CHILDREN
                target[first : first + CHILDREN, column] = cosine * real + sine * imag
                first = first + children
                target[first : first + CHILDREN, column] = cosine * imag - sine * real

    def multiply(index, b):
        at = pl.multiple_of(jnp.minimum(index, end) * 2 * LANES, 2 * LANES)
        weight = w_ref[:, pl.ds(at, 2 * LANES)]
        source = stages[b % 2]
        both = contract(split(source[...]), band(weight, picks), (1, 1))
        mains[b % 2] = both[:, :LANES]
        rim_ref[b % 4] = both[:, LANES:]

    @pl.when(step == 0)
    def _():
        for k in range(total):
            fields[me ^ k] = sources[k][...].reshape(parents * rows_of, LANES)
        stage(jnp.int32(0), 0)
        multiply(jnp.int32(0), 0)
        stage(jnp.int32(1), 1)
        rim_ref[3] = jnp.zeros((rows, LANES), jnp.float32)
        low_ref[...] = narrow(rim_ref[0], LANES - 8)

    inside = jnp.where(step < total - 1, 1.0, 0.0).astype(jnp.float32)
    first = step * blocks
    for b in range(1, blocks + 1):
        multiply(first + b, b)
        stage(first + b + 1, b + 1)
        columns = slice(LANES * (b - 1), LANES * b)
        after = rim_ref[b % 4] * inside if b == blocks else rim_ref[b % 4]
        value = mains[(b - 1) % 2] + jnp.where(lane < LANES // 2, rim_ref[(b - 2) % 4], after)
        lanes = pl.ds(pl.multiple_of((first + b - 1) * LANES, LANES), LANES)
        out_ref[:, :, columns] = local_ref[:, :, lanes] + value.reshape(comps, children, LANES)

    for b in range(2 * blocks):
        for comp in range(comps):
            for part in range(parents // 8):
                incoming_ref[comp, 8 * part : 8 * part + 8, b * LANES : (b + 1) * LANES] = fields[
                    step, pl.ds(8 * part * rows_of + 2 * b + comp, 8, stride=rows_of), :
                ]

    @pl.when(step == total - 1)
    def _():
        high_ref[...] = narrow(rim_ref[(blocks - 1) % 4], 0)


def spread(me, child_local, weight, phase, sources):
    total = len(sources)
    parents, rows_of, _ = sources[0].shape
    comps, children, width = child_local.shape
    rows = comps * children
    span = width // total
    smem = pl.BlockSpec(memory_space=pltpu.SMEM)
    vmem = pl.BlockSpec(memory_space=pltpu.VMEM)
    rim = pl.BlockSpec((8, rows), lambda g: (0, 0))
    return pl.pallas_call(
        spread_kernel,
        grid=(total,),
        in_specs=[smem] + [vmem] * (3 + total),
        out_specs=[
            pl.BlockSpec((comps, parents, 2 * span), lambda g: (0, 0, g)),
            pl.BlockSpec((comps, children, span), lambda g: (0, 0, g)),
            rim,
            rim,
        ],
        out_shape=[
            jax.ShapeDtypeStruct((comps, parents, 2 * width), jnp.float32),
            jax.ShapeDtypeStruct((comps, children, width), jnp.float32),
            jax.ShapeDtypeStruct((8, rows), jnp.float32),
            jax.ShapeDtypeStruct((8, rows), jnp.float32),
        ],
        scratch_shapes=[
            pltpu.VMEM((total, parents * rows_of, LANES), jnp.float32),
            pltpu.VMEM((rows, 2 * LANES), jnp.float32),
            pltpu.VMEM((rows, 2 * LANES), jnp.float32),
            pltpu.VMEM((2, rows, LANES), jnp.float32),
            pltpu.VMEM((4, rows, LANES), jnp.float32),
        ],
        name="spread",
        compiler_params=GRANT,
        cost_estimate=pl.CostEstimate(flops=8 << 30, bytes_accessed=12 << 20, transcendentals=0),
    )(jnp.full((total,), me, jnp.int32), *on_chip(child_local, weight, phase, *sources))


def join_kernel(from_left_ref, from_right_ref, whole_ref, out_ref, held, arrived, left):
    del whole_ref
    comps, children, width = out_ref.shape
    ends = (0, width - LANES)
    reads = [
        pltpu.make_async_copy(out_ref.at[:, :, at : at + LANES], held.at[i], arrived.at[i])
        for i, at in enumerate(ends)
    ]
    writes = [
        pltpu.make_async_copy(held.at[i], out_ref.at[:, :, at : at + LANES], left.at[i])
        for i, at in enumerate(ends)
    ]
    for read in reads:
        read.start()
    for i, (rim_ref, at) in enumerate(((from_left_ref, 0), (from_right_ref, LANES - 8))):
        added = widen(rim_ref[...], at).reshape(comps, children, LANES)
        reads[i].wait()
        held[i] = held[i] + added
        writes[i].start()
    for write in writes:
        write.wait()


def join(child_incoming, from_left, from_right):
    comps, children, _ = child_incoming.shape
    whole = pl.BlockSpec(memory_space=pl.ANY)
    return pl.pallas_call(
        join_kernel,
        in_specs=[pl.BlockSpec(memory_space=pltpu.VMEM)] * 2 + [whole],
        out_specs=whole,
        out_shape=jax.ShapeDtypeStruct(child_incoming.shape, jnp.float32),
        input_output_aliases={2: 0},
        scratch_shapes=[
            pltpu.VMEM((2, comps, children, LANES), jnp.float32),
            pltpu.SemaphoreType.DMA((2,)),
            pltpu.SemaphoreType.DMA((2,)),
        ],
        name="join",
        compiler_params=GRANT,
        cost_estimate=pl.CostEstimate(flops=1 << 20, bytes_accessed=1 << 19, transcendentals=0),
    )(*on_chip(from_left, from_right), child_incoming)


def ring(count):
    forward = [(i, (i + 1) % count) for i in range(count)]
    return forward, [(target, source) for source, target in forward]


def fast(
    child_pattern,
    child_local,
    interp_weight,
    child_phase,
    translator,
    partners,
    operator_id,
    list_len,
):
    total = lax.axis_size("cluster")
    me = lax.axis_index("cluster")
    before, after = exchange(*rims(child_pattern))

    def swap(block, k):
        if k == 0:
            return block
        return lax.ppermute(block, "cluster", [(i, i ^ k) for i in range(total)])

    sent = [None] * total
    for ks in gathers(total):
        made = aggregate(me, total, ks, child_pattern, before, after, interp_weight, child_phase)
        for k, block in zip(ks, made):
            sent[k] = block
    sources = [swap(sent[k], k) for k in range(total)]

    translator, partners, operator_id, list_len, _ = lax.optimization_barrier(
        (translator, partners, operator_id, list_len, sent[0])
    )
    count, comps, samples = translator.shape
    table = translator.reshape(count, comps, samples // LANES, LANES).transpose(0, 2, 1, 3)
    table = table.reshape(count, comps * samples // LANES, LANES)
    rows = comps * samples // LANES // total
    table = lax.dynamic_slice_in_dim(table, me * rows, rows, 1)
    table = jnp.pad(table, ((0, 1), (0, 0), (0, 0)))
    lists = plan(partners, operator_id, list_len, count, rows)
    back = translate(me, lists, table, sources)
    fields = [swap(back[k], k) for k in range(total)]
    incoming, child_incoming, low, high = spread(
        me, child_local, interp_weight, child_phase, fields
    )
    from_left, from_right = exchange(high, low)
    return incoming, join(child_incoming, from_left, from_right)


def gathers(total):
    if total == 8:
        return (7, 6, 5, 3), (2, 4, 1, 0)
    order = tuple(range(total - 1, -1, -1))
    return (order[: total // 2], order[total // 2 :])


def with_halo(block, sides, width):
    for axis, dim in sides:
        forward, backward = ring(lax.axis_size(axis))
        low = lax.ppermute(
            lax.slice_in_dim(block, block.shape[dim] - width, None, axis=dim), axis, forward
        )
        high = lax.ppermute(lax.slice_in_dim(block, 0, width, axis=dim), axis, backward)
        block = jnp.concatenate([low, block, high], axis=dim)
    return block


def translate_rows(pattern, table, partner_rows, operator_rows, lengths):
    receivers = partner_rows.shape[0]
    slot_count = partner_rows.shape[1]
    group_size = 16
    sample_count = pattern.shape[2]

    def advance(block, total):
        partner_cols = lax.dynamic_slice_in_dim(partner_rows, block * group_size, group_size, 1)
        operator_cols = lax.dynamic_slice_in_dim(operator_rows, block * group_size, group_size, 1)
        slot_index = block * group_size + jnp.arange(group_size)
        alive_mask = (slot_index[None, :] < lengths[:, None]).astype(jnp.float32)
        source = jnp.take(pattern, partner_cols, axis=1)
        coupling = jnp.take(table, operator_cols, axis=0)
        coup_real = coupling[:, :, 0] * alive_mask[:, :, None]
        coup_imag = coupling[:, :, 1] * alive_mask[:, :, None]
        real_part = jnp.sum(coup_real * source[0] - coup_imag * source[1], axis=1)
        imag_part = jnp.sum(coup_real * source[1] + coup_imag * source[0], axis=1)
        return total + jnp.stack([real_part, imag_part])

    start_total = jnp.zeros((2, receivers, sample_count), jnp.float32)
    return lax.fori_loop(0, slot_count // group_size, advance, start_total)


def phase_sum(upsampled, cosine, sine, parent_count):
    grouped = upsampled.reshape(2, parent_count, CHILDREN, upsampled.shape[2])
    real_part = jnp.sum(cosine[None] * grouped[0] - sine[None] * grouped[1], axis=1)
    imag_part = jnp.sum(cosine[None] * grouped[1] + sine[None] * grouped[0], axis=1)
    return jnp.stack([real_part, imag_part])


def phase_spread(incoming, cosine, sine):
    shifted_real = cosine[None] * incoming[0][:, None] + sine[None] * incoming[1][:, None]
    shifted_imag = cosine[None] * incoming[1][:, None] - sine[None] * incoming[0][:, None]
    return jnp.stack([shifted_real, shifted_imag]).reshape(2, -1, incoming.shape[2])


def plain(
    child_pattern,
    child_local,
    interp_weight,
    child_phase,
    translator,
    partners,
    operator_id,
    list_len,
):
    rim_width = TAPS // 2
    child_count = child_pattern.shape[1]
    parent_count = child_count // CHILDREN
    half_samples = child_pattern.shape[2]
    cosine = jnp.cos(child_phase)
    sine = jnp.sin(child_phase)
    cos_even = cosine[:, 0::2]
    cos_odd = cosine[:, 1::2]
    sin_even = sine[:, 0::2]
    sin_odd = sine[:, 1::2]
    weight_even = interp_weight[:, 0::2]
    weight_odd = interp_weight[:, 1::2]
    padded = with_halo(child_pattern, (("sample", 2),), rim_width)
    up_even = jnp.zeros((2, child_count, half_samples), jnp.float32)
    up_odd = jnp.zeros((2, child_count, half_samples), jnp.float32)
    for tap in range(TAPS):
        window = padded[:, :, 1 + tap : 1 + tap + half_samples]
        up_even = up_even + weight_even[tap][None, None, :] * window
        up_odd = up_odd + weight_odd[tap][None, None, :] * window
    parent_even = phase_sum(up_even, cos_even, sin_even, parent_count)
    parent_odd = phase_sum(up_odd, cos_odd, sin_odd, parent_count)
    parent = jnp.stack([parent_even, parent_odd], axis=3).reshape(2, parent_count, 2 * half_samples)
    cluster_index = lax.axis_index("cluster")
    whole = lax.all_gather(parent, "cluster", axis=1, tiled=True)
    first_row = cluster_index * parent_count
    own_partners = lax.dynamic_slice_in_dim(partners, first_row, parent_count, 0)
    own_operators = lax.dynamic_slice_in_dim(operator_id, first_row, parent_count, 0)
    own_lengths = lax.dynamic_slice_in_dim(list_len, first_row, parent_count, 0)
    incoming = translate_rows(whole, translator, own_partners, own_operators, own_lengths)
    shift_even = phase_spread(incoming[:, :, 0::2], cos_even, sin_even)
    shift_odd = phase_spread(incoming[:, :, 1::2], cos_odd, sin_odd)
    weighted = jnp.stack(
        [
            weight_even[tap][None, None, :] * shift_even
            + weight_odd[tap][None, None, :] * shift_odd
            for tap in range(TAPS)
        ]
    )
    padded_weighted = with_halo(weighted, (("sample", 3),), rim_width)
    child_incoming = child_local
    for tap in range(TAPS):
        offset = 2 * rim_width - 1 - tap
        child_incoming = child_incoming + padded_weighted[tap, :, :, offset : offset + half_samples]
    return (incoming, child_incoming)


def fits(width, total):
    share = width // total
    even = total > 1 and total & (total - 1) == 0 and share * total == width
    return even and share >= 4 * LANES and share % (4 * LANES) == 0


def local(child_pattern, *rest):
    if fits(child_pattern.shape[2], lax.axis_size("cluster")):
        return fast(child_pattern, *rest)
    return plain(child_pattern, *rest)


def solution(mesh):
    placed = (
        P(None, "cluster", "sample"),
        P(None, "cluster", "sample"),
        P(None, "sample"),
        P(None, "sample"),
        P(None, None, "sample"),
        P(),
        P(),
        P(),
    )
    return jax.shard_map(
        local,
        mesh=mesh,
        in_specs=placed,
        out_specs=(P(None, "cluster", "sample"), P(None, "cluster", "sample")),
        check_vma=False,
    )
```
